128 devices in a mesh: ctx: 16 (over z, y), ch: 8 (over x, core).
Axes of the slice: x: 4, y: 4, z: 4, core: 2. Of those that a mesh axis runs over, the one named last changes fastest.
Arguments:
- outer_gate: bfloat16 [4096, 4096], P('ctx', 'ch'), may hold values from -6 to 6
- inner_gate: bfloat16 [4096, 4096], P('ctx', 'ch'), may hold values from -6 to 6
- values_in: bfloat16 [4096, 4096], P('ctx', 'ch'), may hold values from -6 to 6
- filters: float32 [4096, 4096], P('ctx', 'ch'), as said below
- skip_gain: float32 [4096], P('ch'), may hold values from 0.5 to 1.5
- w_out: bfloat16 [4096, 4096], P('ch', 'ctx'), may hold values from -0.125 to 0.125
Outputs:
- mixed: bfloat16 [4096, 4096], P('ctx', 'ch')
The draws below stay inside these ranges and needn't reach their ends.
Inputs may be any that keep to these rules, and one draw needn't show every extreme that they name: `filters`: finite values.
All inputs are finite; a program needn't handle non-finite values.
Results may differ from the reference program's by a relative error of at most 0.022.
Values may be sent and summed in bfloat16 or wider, within the bound.
A program may use at most 64 MiB of HBM per device.

```python
import math
import jax
import jax.numpy as jnp

D = 4096
SEQ = 4096


def draw_filters(key, part):
    key_tau = jax.random.fold_in(key, 0)
    key_noise = jax.random.fold_in(key, 1)
    key_slow = jax.random.fold_in(key, 3)
    key_share = jax.random.fold_in(key, 4)
    key_far = jax.random.fold_in(key, 5)
    lags = jnp.arange(SEQ, dtype=jnp.float32)[:, None]
    log_tau = jax.random.uniform(key_tau, (D,), jnp.float32, math.log(30.0), math.log(4.0 * SEQ))
    noise = jax.random.normal(key_noise, (SEQ, D), jnp.float32)
    far_noise = jax.random.normal(key_far, (SEQ, D), jnp.float32)
    scale = jnp.ones((D,), jnp.float32)
    tau = jnp.exp(log_tau)
    slow_tau = jnp.exp(jax.random.uniform(key_slow, (D,), jnp.float32, math.log(2.0 * SEQ), math.log(8.0 * SEQ)))
    slow_share = jnp.exp(jax.random.uniform(key_share, (D,), jnp.float32, math.log(0.5), 0.0))
    amplitude = scale / jnp.sqrt(jnp.minimum(tau, float(SEQ)))
    slow_amplitude = slow_share / math.sqrt(float(SEQ))
    fast_mode = amplitude[None, :] * jnp.exp(-lags / tau[None, :]) * noise
    slow_mode = slow_amplitude[None, :] * jnp.exp(-lags / slow_tau[None, :]) * far_noise
    return (fast_mode + slow_mode).astype(jnp.float32)


def strengthened(drawn, own_key, source, target, blocks, factor):
    owner, partner = [(jnp.arange(drawn.shape[axis_at]) // (drawn.shape[axis_at] // blocks)).reshape([-1 if axis == axis_at else 1 for axis in range(drawn.ndim)]) for axis_at in (source, target)]
    chosen = jax.random.permutation(own_key, blocks)[partner]
    strong = (owner == chosen) | (owner == (partner + blocks // 2) % blocks)
    return jnp.where(strong, factor * drawn, drawn)


def block_levels(stream_key, shape, pieces, least, largest):
    def one(position, parts):
        heights = jax.random.uniform(jax.random.fold_in(jax.random.fold_in(stream_key, 6), position), (parts,), jnp.float32, least / len(pieces), largest / len(pieces))
        return jnp.repeat(jnp.exp(heights), shape[position] // parts).reshape((-1,) + (1,) * (len(shape) - position - 1))

    factor_of = one(*pieces[0])
    for cut in pieces[1:]:
        factor_of = factor_of * one(*cut)
    return factor_of


def bell_draw(rng, extent, scale, reach, cuts=(), kind=jnp.bfloat16):
    entries = scale * jax.random.normal(rng, extent, jnp.float32)
    if cuts:
        entries = entries * block_levels(rng, extent, cuts, -0.22, 0.18)
    return jnp.clip(entries, -reach, reach).astype(kind)


def bell_draw_with(stream_key, dims, deviation, limit, cuts, heavy, held_as=jnp.bfloat16):
    drawn = deviation * jax.random.normal(stream_key, dims, jnp.float32)
    if cuts:
        drawn = drawn * block_levels(stream_key, dims, cuts, -0.22, 0.18)
    return jnp.clip(strengthened(drawn, jax.random.fold_in(stream_key, 3), *heavy), -limit, limit).astype(held_as)


def setup_inputs(seed: int = 0) -> dict:
    key_of = jax.random.split(jax.random.key(seed), 7)
    return {
        "outer_gate": bell_draw(key_of[0], (SEQ, D), 1.0, 6.0, ((0, 16), (1, 8))),
        "inner_gate": bell_draw(key_of[1], (SEQ, D), 1.0, 6.0, ((0, 16), (1, 8))),
        "values_in": bell_draw(key_of[2], (SEQ, D), 1.0, 6.0, ((0, 16), (1, 8))),
        "filters": draw_filters(jax.random.fold_in(key_of[6], 71), 0),
        "skip_gain": jnp.clip(0.5 + 1.0 * jax.random.uniform(key_of[4], (D,), jnp.float32) ** block_levels(key_of[4], (D,), ((0, 8),), -0.2, 0.2), 0.5, 1.5),
        "w_out": bell_draw_with(key_of[5], (D, D), D ** -0.5, 0.125, ((0, 8), (1, 16)), (0, 1, 16, 2.0)),
    }


def reference(outer_gate, inner_gate, values_in, filters, skip_gain, w_out):
    gated = (inner_gate.astype(jnp.float32) * values_in.astype(jnp.float32)).astype(jnp.bfloat16)
    gated_f = gated.astype(jnp.float32)
    length = 2 * SEQ
    spec_in = jnp.fft.rfft(gated_f, n=length, axis=0)
    spec_filter = jnp.fft.rfft(filters, n=length, axis=0)
    conv = jnp.fft.irfft(spec_in * spec_filter, n=length, axis=0)[:SEQ]
    mix_in = (outer_gate.astype(jnp.float32) * (conv + skip_gain[None, :] * gated_f)).astype(jnp.bfloat16)
    return jnp.dot(mix_in, w_out, preferred_element_type=jnp.float32).astype(jnp.bfloat16)
```

```python
import functools

import jax
import jax.numpy as jnp
import numpy as np
from jax import lax
from jax.experimental import pallas as pl
from jax.experimental.pallas import tpu as pltpu
from jax.sharding import PartitionSpec as P

BF16 = jnp.bfloat16
F32 = jnp.float32
RING = 4


def forward_table(block):
    place = np.arange(block, dtype=np.int64)[:, None]
    freq = np.arange(block, dtype=np.int64)[None, :]
    angle = np.pi / (2 * block) * (place * (2 * freq + 1) % (4 * block)).astype(np.float64)
    return np.concatenate([np.cos(angle), -np.sin(angle)], axis=1).astype(jnp.bfloat16)


def inverse_table(block):
    freq = np.arange(block, dtype=np.int64)[:, None]
    place = np.arange(2 * block, dtype=np.int64)[None, :]
    angle = np.pi / (2 * block) * (place * (2 * freq + 1) % (4 * block)).astype(np.float64)
    return (np.concatenate([np.cos(angle), -np.sin(angle)], axis=0) / block).astype(jnp.bfloat16)


def kernel(
    og_h, ig_h, vi_h, fl_h, sk_ref, w_h, ft_h, it_h, out_ref,
    og, ig, vi, fl, ft, it, gated, gsend, hsend, gx, hx, gs, hs, ys, ps, csend, cx, mix, wall,
    part, other, cr, s1, r1, s2, r2,
    ld, gsem_s, gsem_r, hsem_s, hsem_r, csem_s, csem_r, wsem_s, wsem_r, osem_s, osem_r, xsem_s, xsem_r,
):
    nctx = 16
    me = lax.axis_index("ctx")
    mych = lax.axis_index("ch")
    y, z = lax.rem(me, RING), me // RING
    x, core = mych // 2, lax.rem(mych, 2)
    sub = gsend.shape[0] // nctx
    half = w_h.shape[0] // 2

    def ctx_of(ry, rz):
        return lax.rem(z + rz + RING, RING) * RING + lax.rem(y + ry + RING, RING)

    def ch_of(rx, c):
        return lax.rem(x + rx + RING, RING) * 2 + c

    loads = [
        pltpu.make_async_copy(src, dst, ld.at[n])
        for n, (src, dst) in enumerate(
            [(ig_h, ig), (vi_h, vi), (fl_h, fl), (w_h, wall.at[me]), (ft_h, ft), (it_h, it), (og_h, og)]
        )
    ]
    for copy in loads:
        copy.start()

    barrier = pltpu.get_barrier_semaphore()
    for d in range(1, nctx):
        pl.semaphore_signal(barrier, inc=1, device_id={"ctx": lax.rem(me + d, nctx)})
    pl.semaphore_signal(barrier, inc=1, device_id={"ch": ch_of(0, 1 - core)})
    pl.semaphore_signal(barrier, inc=1, device_id={"ch": ch_of(1, core)})
    pl.semaphore_signal(barrier, inc=1, device_id={"ch": ch_of(-1, core)})

    sent = []
    kinds = {}

    def w_copy(h, stage, ra, what):
        key = (h, stage, ra, what)
        if key not in kinds:
            kinds[key] = len(kinds)
        n = kinds[key]
        step = 1 if what in ("R", "FR") else -1
        rel = {"R": 0, "L": 0, "FR": -1, "FL": 1}[what]
        rows = {"R": (0, half), "L": (0, half), "FR": (0, half // 2), "FL": (half // 2, half // 2)}[what]
        first, second = (rel, 0) if stage == 0 else (ra, rel)
        chunk = ctx_of(first, second) if h == 0 else ctx_of(second, first)
        along_y = (h == 0) == (stage == 0)
        to = ctx_of(step, 0) if along_y else ctx_of(0, step)
        ref = wall.at[chunk, pl.ds(h * half + rows[0], rows[1])]
        return pltpu.make_async_remote_copy(
            src_ref=ref, dst_ref=ref, send_sem=wsem_s.at[n], recv_sem=wsem_r.at[n], device_id={"ctx": to}
        )

    def w_wait(h, stage, ra, what):
        n = kinds[(h, stage, ra, what)]
        step = 1 if what in ("R", "FR") else -1
        rel = {"R": 0, "L": 0, "FR": -1, "FL": 1}[what] - step
        rows = {"R": (0, half), "L": (0, half), "FR": (0, half // 2), "FL": (half // 2, half // 2)}[what]
        first, second = (rel, 0) if stage == 0 else (ra, rel)
        chunk = ctx_of(first, second) if h == 0 else ctx_of(second, first)
        along_y = (h == 0) == (stage == 0)
        to = ctx_of(step, 0) if along_y else ctx_of(0, step)
        ref = wall.at[chunk, pl.ds(h * half + rows[0], rows[1])]
        pltpu.make_async_remote_copy(
            src_ref=ref, dst_ref=ref, send_sem=wsem_s.at[n], recv_sem=wsem_r.at[n], device_id={"ctx": to}
        ).wait_recv()

    def w_send(h, stage, ra, what):
        copy = w_copy(h, stage, ra, what)
        copy.start()
        sent.append(copy)

    def exchange(src, dst, ssem, rsem, d):
        to = lax.rem(me + d, nctx)
        return pltpu.make_async_remote_copy(
            src_ref=src.at[pl.ds(pl.multiple_of(to * sub, sub), sub)],
            dst_ref=dst.at[pl.ds(pl.multiple_of(me * sub, sub), sub)],
            send_sem=ssem.at[d],
            recv_sem=rsem.at[d],
            device_id={"ctx": to},
        )

    def exchange_wait(src, dst, ssem, rsem, d):
        frm = lax.rem(me - d + nctx, nctx)
        pltpu.make_async_remote_copy(
            src_ref=src.at[pl.ds(pl.multiple_of(frm * sub, sub), sub)],
            dst_ref=dst.at[pl.ds(pl.multiple_of(frm * sub, sub), sub)],
            send_sem=ssem.at[d],
            recv_sem=rsem.at[d],
            device_id={"ctx": frm},
        ).wait_recv()

    def exchange_all(src, dst, ssem, rsem):
        for d in range(1, nctx):
            copy = exchange(src, dst, ssem, rsem, d)
            copy.start()
            sent.append(copy)
        mine = pl.ds(pl.multiple_of(me * sub, sub), sub)
        dst[mine, :] = src[mine, :]

    loads[0].wait()
    loads[1].wait()
    product = (ig[...].astype(F32) * vi[...].astype(F32)).astype(BF16)
    gated[...] = product
    gsend[...] = jnp.transpose(product.astype(F32)).astype(BF16)
    loads[3].wait()
    pl.semaphore_wait(barrier, nctx + 2)
    exchange_all(gsend, gx, gsem_s, gsem_r)
    loads[2].wait()
    hsend[...] = jnp.transpose(fl[...]).astype(BF16)
    exchange_all(hsend, hx, hsem_s, hsem_r)
    for h in (0, 1):
        for what in ("R", "L"):
            w_send(h, 0, 0, what)
    for h in (0, 1):
        for what in ("R", "L"):
            w_send(h, 1, 0, what)

    loads[4].wait()
    for d in range(1, nctx):
        exchange_wait(gsend, gx, gsem_s, gsem_r, d)
    gs[...] = jnp.dot(gx[...], ft[...], preferred_element_type=F32)
    for d in range(1, nctx):
        exchange_wait(hsend, hx, hsem_s, hsem_r, d)
    hs[...] = jnp.dot(hx[...], ft[...], preferred_element_type=F32)

    for h in (0, 1):
        w_wait(h, 0, 0, "R")
        w_send(h, 0, 0, "FR")
        w_send(h, 1, -1, "R")
        w_send(h, 1, -1, "L")
        w_wait(h, 0, 0, "L")
        w_send(h, 0, 0, "FL")
        w_send(h, 1, 1, "R")
        w_send(h, 1, 1, "L")

    bins = gs.shape[1] // 2

    def block_products(n, carry):
        row = pl.multiple_of(n * 8, 8)
        for lane in range(0, bins, 128):
            gr = [gs[pl.ds(b * sub + row, 8), pl.ds(lane, 128)] for b in range(nctx)]
            gi = [gs[pl.ds(b * sub + row, 8), pl.ds(bins + lane, 128)] for b in range(nctx)]
            hr = [hs[pl.ds(b * sub + row, 8), pl.ds(lane, 128)] for b in range(nctx)]
            hi = [hs[pl.ds(b * sub + row, 8), pl.ds(bins + lane, 128)] for b in range(nctx)]
            for i in range(nctx):
                re = gr[0] * hr[i] - gi[0] * hi[i]
                im = gr[0] * hi[i] + gi[0] * hr[i]
                for j in range(1, i + 1):
                    re += gr[j] * hr[i - j] - gi[j] * hi[i - j]
                    im += gr[j] * hi[i - j] + gi[j] * hr[i - j]
                ys[pl.ds(i * sub + row, 8), pl.ds(lane, 128)] = re
                ys[pl.ds(i * sub + row, 8), pl.ds(bins + lane, 128)] = im
        return carry

    lax.fori_loop(0, sub // 8, block_products, 0)

    loads[5].wait()
    ps[...] = jnp.dot(ys[...].astype(BF16), it[...], preferred_element_type=F32)
    csend[pl.ds(0, sub), :] = ps[pl.ds(0, sub), pl.ds(0, bins)].astype(BF16)
    rest = sub * (nctx - 1)
    csend[pl.ds(sub, rest), :] = (
        ps[pl.ds(sub, rest), pl.ds(0, bins)] + ps[pl.ds(0, rest), pl.ds(bins, bins)]
    ).astype(BF16)
    exchange_all(csend, cx, csem_s, csem_r)

    for h in (0, 1):
        w_wait(h, 0, 0, "FR")
        w_wait(h, 0, 0, "FL")
        w_send(h, 1, 2, "R")
        w_send(h, 1, 2, "L")
    for ra in (0, -1, 1):
        for h in (0, 1):
            w_wait(h, 1, ra, "R")
            w_send(h, 1, ra, "FR")
            w_wait(h, 1, ra, "L")
            w_send(h, 1, ra, "FL")

    loads[6].wait()
    for d in range(1, nctx):
        exchange_wait(csend, cx, csem_s, csem_r, d)
    conv = jnp.transpose(cx[...].astype(F32))
    mix[...] = (og[...].astype(F32) * (conv + sk_ref[...] * gated[...].astype(F32))).astype(BF16)

    for ra in (2,):
        for h in (0, 1):
            w_wait(h, 1, ra, "R")
            w_send(h, 1, ra, "FR")
            w_wait(h, 1, ra, "L")
            w_send(h, 1, ra, "FL")
    for ra in (0, -1, 1, 2):
        for h in (0, 1):
            w_wait(h, 1, ra, "FR")
            w_wait(h, 1, ra, "FL")

    cols = w_h.shape[1]

    def columns(rx, c, n):
        q = lax.rem(x + rx + RING, RING)
        return jnp.dot(mix[...], wall[q * RING + c * 2 + n], preferred_element_type=F32)

    turns = (2, 1, -1, 0)
    swaps = []
    for k, rx in enumerate(turns):
        for n in (0, 1):
            other[k, :, n * cols : (n + 1) * cols] = columns(rx, 1 - core, n).astype(BF16)
        copy = pltpu.make_async_remote_copy(
            src_ref=other.at[k], dst_ref=cr.at[k], send_sem=osem_s.at[k], recv_sem=osem_r.at[k],
            device_id={"ch": ch_of(0, 1 - core)},
        )
        copy.start()
        swaps.append(copy)
    for k, rx in enumerate(turns):
        for n in (0, 1):
            part[k, :, n * cols : (n + 1) * cols] = columns(rx, core, n)

    rows = mix.shape[0]
    top, low = pl.ds(0, rows // 2), pl.ds(rows // 2, rows // 2)

    def ring(n, src, dst, step):
        copy = pltpu.make_async_remote_copy(
            src_ref=src, dst_ref=dst, send_sem=xsem_s.at[n], recv_sem=xsem_r.at[n],
            device_id={"ch": ch_of(step, core)},
        )
        copy.start()
        return copy

    swaps[0].wait_recv()
    s1[...] = (part[0] + cr[0].astype(F32)).astype(BF16)
    up1 = ring(0, s1.at[top], r1.at[top], 1)
    down1 = ring(1, s1.at[low], r1.at[low], -1)
    swaps[1].wait_recv()
    s2[0, low, :] = (part[1, low, :] + cr[1, low, :].astype(F32)).astype(BF16)
    up2 = ring(2, s2.at[0, low], r2.at[0, low], 1)
    swaps[2].wait_recv()
    s2[1, top, :] = (part[2, top, :] + cr[2, top, :].astype(F32)).astype(BF16)
    down2 = ring(3, s2.at[1, top], r2.at[1, top], -1)
    up1.wait_recv()
    s2[0, top, :] = (part[1, top, :] + cr[1, top, :].astype(F32) + r1[top, :].astype(F32)).astype(BF16)
    up3 = ring(4, s2.at[0, top], r2.at[0, top], 1)
    down1.wait_recv()
    s2[1, low, :] = (part[2, low, :] + cr[2, low, :].astype(F32) + r1[low, :].astype(F32)).astype(BF16)
    down3 = ring(5, s2.at[1, low], r2.at[1, low], -1)
    swaps[3].wait_recv()
    part[3] = part[3] + cr[3].astype(F32)
    for copy in (up2, down2, up3, down3):
        copy.wait_recv()
    out_ref[...] = (part[3] + r2[0].astype(F32) + r2[1].astype(F32)).astype(BF16)

    for copy in sent + swaps + [up1, down1, up2, down2, up3, down3]:
        copy.wait_send()


def per_device(outer_gate, inner_gate, values_in, filters, skip_gain, w_out):
    rows, chans = outer_gate.shape
    depth, cols = w_out.shape
    nctx = 16
    hbm = pl.BlockSpec(memory_space=pl.ANY)
    vmem = pl.BlockSpec(memory_space=pltpu.VMEM)
    dma = pltpu.SemaphoreType.DMA
    scratch = [
        pltpu.VMEM((rows, chans), BF16),
        pltpu.VMEM((rows, chans), BF16),
        pltpu.VMEM((rows, chans), BF16),
        pltpu.VMEM((rows, chans), F32),
        pltpu.VMEM((rows, 2 * rows), BF16),
        pltpu.VMEM((2 * rows, 2 * rows), BF16),
        pltpu.VMEM((rows, chans), BF16),
        pltpu.VMEM((chans, rows), BF16),
        pltpu.VMEM((chans, rows), BF16),
        pltpu.VMEM((chans, rows), BF16),
        pltpu.VMEM((chans, rows), BF16),
        pltpu.VMEM((chans, 2 * rows), F32),
        pltpu.VMEM((chans, 2 * rows), F32),
        pltpu.VMEM((chans, 2 * rows), F32),
        pltpu.VMEM((chans, 2 * rows), F32),
        pltpu.VMEM((chans, rows), BF16),
        pltpu.VMEM((chans, rows), BF16),
        pltpu.VMEM((rows, chans), BF16),
        pltpu.VMEM((nctx, depth, cols), BF16),
        pltpu.VMEM((RING, rows, 2 * cols), F32),
        pltpu.VMEM((RING, rows, 2 * cols), BF16),
        pltpu.VMEM((RING, rows, 2 * cols), BF16),
        pltpu.VMEM((rows, 2 * cols), BF16),
        pltpu.VMEM((rows, 2 * cols), BF16),
        pltpu.VMEM((2, rows, 2 * cols), BF16),
        pltpu.VMEM((2, rows, 2 * cols), BF16),
        dma((7,)),
        dma((nctx,)), dma((nctx,)), dma((nctx,)), dma((nctx,)), dma((nctx,)), dma((nctx,)),
        dma((40,)), dma((40,)),
        dma((RING,)), dma((RING,)),
        dma((6,)), dma((6,)),
    ]
    return pl.pallas_call(
        kernel,
        out_shape=jax.ShapeDtypeStruct((rows, chans), BF16),
        in_specs=[hbm, hbm, hbm, hbm, vmem, hbm, hbm, hbm],
        out_specs=vmem,
        scratch_shapes=scratch,
        compiler_params=pltpu.CompilerParams(
            collective_id=0, has_side_effects=True, vmem_limit_bytes=48 * 1024 * 1024
        ),
        name="long_conv_layer",
    )(
        outer_gate, inner_gate, values_in, filters, skip_gain[None, :], w_out,
        jnp.asarray(forward_table(rows)), jnp.asarray(inverse_table(rows)),
    )


def solution(mesh):
    placed = (
        P("ctx", "ch"),
        P("ctx", "ch"),
        P("ctx", "ch"),
        P("ctx", "ch"),
        P("ch"),
        P("ch", "ctx"),
    )
    return jax.shard_map(
        per_device, mesh=mesh, in_specs=placed, out_specs=P("ctx", "ch"), check_vma=False
    )
```

```python
import functools

import jax
import jax.numpy as jnp
import numpy as np
from jax import lax
from jax.experimental import pallas as pl
from jax.experimental.pallas import tpu as pltpu
from jax.sharding import PartitionSpec as P

BF16 = jnp.bfloat16
F32 = jnp.float32
RING = 4


def forward_table(block):
    place = np.arange(block, dtype=np.int64)[:, None]
    freq = np.arange(block, dtype=np.int64)[None, :]
    angle = np.pi / (2 * block) * (place * (2 * freq + 1) % (4 * block)).astype(np.float64)
    return np.concatenate([np.cos(angle), -np.sin(angle)], axis=1).astype(jnp.bfloat16)


def inverse_table(block):
    freq = np.arange(block, dtype=np.int64)[:, None]
    place = np.arange(2 * block, dtype=np.int64)[None, :]
    angle = np.pi / (2 * block) * (place * (2 * freq + 1) % (4 * block)).astype(np.float64)
    return (np.concatenate([np.cos(angle), -np.sin(angle)], axis=0) / block).astype(jnp.bfloat16)


def kernel(
    og_h, ig_h, vi_h, fl_h, sk_h, w_h, ft_h, it_h, out_ref,
    og, ig, vi, fl, sk, ft, it, gated, gsend, hsend, gx, hx, gs, hs, ys, ps, csend, cx, mix, wall,
    part, other, cr, s1, r1, s2, r2,
    ld, gsem_s, gsem_r, hsem_s, hsem_r, csem_s, csem_r, wsem_s, wsem_r, osem_s, osem_r, xsem_s, xsem_r,
):
    nctx = 16
    me = lax.axis_index("ctx")
    mych = lax.axis_index("ch")
    y, z = lax.rem(me, RING), me // RING
    x, core = mych // 2, lax.rem(mych, 2)
    sub = gsend.shape[0] // nctx
    half = w_h.shape[0] // 2

    def ctx_of(ry, rz):
        return lax.rem(z + rz + RING, RING) * RING + lax.rem(y + ry + RING, RING)

    def ch_of(rx, c):
        return lax.rem(x + rx + RING, RING) * 2 + c

    loads = [
        pltpu.make_async_copy(src, dst, ld.at[n])
        for n, (src, dst) in enumerate(
            [(ig_h, ig), (vi_h, vi), (fl_h, fl), (w_h, wall.at[me]), (ft_h, ft), (it_h, it), (og_h, og), (sk_h, sk)]
        )
    ]
    for copy in loads:
        copy.start()

    barrier = pltpu.get_barrier_semaphore()
    for d in range(1, nctx):
        pl.semaphore_signal(barrier, inc=1, device_id={"ctx": lax.rem(me + d, nctx)})
    pl.semaphore_signal(barrier, inc=1, device_id={"ch": ch_of(0, 1 - core)})
    pl.semaphore_signal(barrier, inc=1, device_id={"ch": ch_of(1, core)})
    pl.semaphore_signal(barrier, inc=1, device_id={"ch": ch_of(-1, core)})

    sent = []
    kinds = {}

    def w_copy(h, stage, ra, what):
        key = (h, stage, ra, what)
        if key not in kinds:
            kinds[key] = len(kinds)
        n = kinds[key]
        step = 1 if what in ("R", "FR") else -1
        rel = {"R": 0, "L": 0, "FR": -1, "FL": 1}[what]
        rows = {"R": (0, half), "L": (0, half), "FR": (0, half // 2), "FL": (half // 2, half // 2)}[what]
        first, second = (rel, 0) if stage == 0 else (ra, rel)
        chunk = ctx_of(first, second) if h == 0 else ctx_of(second, first)
        along_y = (h == 0) == (stage == 0)
        to = ctx_of(step, 0) if along_y else ctx_of(0, step)
        ref = wall.at[chunk, pl.ds(h * half + rows[0], rows[1])]
        return pltpu.make_async_remote_copy(
            src_ref=ref, dst_ref=ref, send_sem=wsem_s.at[n], recv_sem=wsem_r.at[n], device_id={"ctx": to}
        )

    def w_wait(h, stage, ra, what):
        n = kinds[(h, stage, ra, what)]
        step = 1 if what in ("R", "FR") else -1
        rel = {"R": 0, "L": 0, "FR": -1, "FL": 1}[what] - step
        rows = {"R": (0, half), "L": (0, half), "FR": (0, half // 2), "FL": (half // 2, half // 2)}[what]
        first, second = (rel, 0) if stage == 0 else (ra, rel)
        chunk = ctx_of(first, second) if h == 0 else ctx_of(second, first)
        along_y = (h == 0) == (stage == 0)
        to = ctx_of(step, 0) if along_y else ctx_of(0, step)
        ref = wall.at[chunk, pl.ds(h * half + rows[0], rows[1])]
        pltpu.make_async_remote_copy(
            src_ref=ref, dst_ref=ref, send_sem=wsem_s.at[n], recv_sem=wsem_r.at[n], device_id={"ctx": to}
        ).wait_recv()

    def w_send(h, stage, ra, what):
        copy = w_copy(h, stage, ra, what)
        copy.start()
        sent.append(copy)

    def exchange(src, dst, ssem, rsem, d):
        to = lax.rem(me + d, nctx)
        return pltpu.make_async_remote_copy(
            src_ref=src.at[pl.ds(pl.multiple_of(to * sub, sub), sub)],
            dst_ref=dst.at[pl.ds(pl.multiple_of(me * sub, sub), sub)],
            send_sem=ssem.at[d],
            recv_sem=rsem.at[d],
            device_id={"ctx": to},
        )

    def exchange_wait(src, dst, ssem, rsem, d):
        frm = lax.rem(me - d + nctx, nctx)
        pltpu.make_async_remote_copy(
            src_ref=src.at[pl.ds(pl.multiple_of(frm * sub, sub), sub)],
            dst_ref=dst.at[pl.ds(pl.multiple_of(frm * sub, sub), sub)],
            send_sem=ssem.at[d],
            recv_sem=rsem.at[d],
            device_id={"ctx": frm},
        ).wait_recv()

    def exchange_all(src, dst, ssem, rsem):
        for d in range(1, nctx):
            copy = exchange(src, dst, ssem, rsem, d)
            copy.start()
            sent.append(copy)
        mine = pl.ds(pl.multiple_of(me * sub, sub), sub)
        dst[mine, :] = src[mine, :]

    loads[0].wait()
    loads[1].wait()
    product = (ig[...].astype(F32) * vi[...].astype(F32)).astype(BF16)
    gated[...] = product
    gsend[...] = jnp.transpose(product.astype(F32)).astype(BF16)
    loads[3].wait()
    pl.semaphore_wait(barrier, nctx + 2)
    exchange_all(gsend, gx, gsem_s, gsem_r)
    loads[2].wait()
    hsend[...] = jnp.transpose(fl[...]).astype(BF16)
    exchange_all(hsend, hx, hsem_s, hsem_r)
    for h in (0, 1):
        for what in ("R", "L"):
            w_send(h, 0, 0, what)
    for h in (0, 1):
        for what in ("R", "L"):
            w_send(h, 1, 0, what)

    loads[4].wait()
    for d in range(1, nctx):
        exchange_wait(gsend, gx, gsem_s, gsem_r, d)
    gs[...] = jnp.dot(gx[...], ft[...], preferred_element_type=F32)
    for d in range(1, nctx):
        exchange_wait(hsend, hx, hsem_s, hsem_r, d)
    hs[...] = jnp.dot(hx[...], ft[...], preferred_element_type=F32)

    for h in (0, 1):
        w_wait(h, 0, 0, "R")
        w_send(h, 0, 0, "FR")
        w_send(h, 1, -1, "R")
        w_send(h, 1, -1, "L")
        w_wait(h, 0, 0, "L")
        w_send(h, 0, 0, "FL")
        w_send(h, 1, 1, "R")
        w_send(h, 1, 1, "L")

    bins = gs.shape[1] // 2

    def block_products(n, carry):
        row = pl.multiple_of(n * 8, 8)
        for lane in range(0, bins, 128):
            gr = [gs[pl.ds(b * sub + row, 8), pl.ds(lane, 128)] for b in range(nctx)]
            gi = [gs[pl.ds(b * sub + row, 8), pl.ds(bins + lane, 128)] for b in range(nctx)]
            hr = [hs[pl.ds(b * sub + row, 8), pl.ds(lane, 128)] for b in range(nctx)]
            hi = [hs[pl.ds(b * sub + row, 8), pl.ds(bins + lane, 128)] for b in range(nctx)]
            for i in range(nctx):
                re = gr[0] * hr[i] - gi[0] * hi[i]
                im = gr[0] * hi[i] + gi[0] * hr[i]
                for j in range(1, i + 1):
                    re += gr[j] * hr[i - j] - gi[j] * hi[i - j]
                    im += gr[j] * hi[i - j] + gi[j] * hr[i - j]
                ys[pl.ds(i * sub + row, 8), pl.ds(lane, 128)] = re
                ys[pl.ds(i * sub + row, 8), pl.ds(bins + lane, 128)] = im
        return carry

    lax.fori_loop(0, sub // 8, block_products, 0)

    loads[5].wait()
    ps[...] = jnp.dot(ys[...].astype(BF16), it[...], preferred_element_type=F32)
    csend[pl.ds(0, sub), :] = ps[pl.ds(0, sub), pl.ds(0, bins)].astype(BF16)
    rest = sub * (nctx - 1)
    csend[pl.ds(sub, rest), :] = (
        ps[pl.ds(sub, rest), pl.ds(0, bins)] + ps[pl.ds(0, rest), pl.ds(bins, bins)]
    ).astype(BF16)
    exchange_all(csend, cx, csem_s, csem_r)

    for h in (0, 1):
        w_wait(h, 0, 0, "FR")
        w_wait(h, 0, 0, "FL")
        w_send(h, 1, 2, "R")
        w_send(h, 1, 2, "L")
    for ra in (0, -1, 1):
        for h in (0, 1):
            w_wait(h, 1, ra, "R")
            w_send(h, 1, ra, "FR")
            w_wait(h, 1, ra, "L")
            w_send(h, 1, ra, "FL")

    loads[6].wait()
    loads[7].wait()
    for d in range(1, nctx):
        exchange_wait(csend, cx, csem_s, csem_r, d)
    conv = jnp.transpose(cx[...].astype(F32))
    mix[...] = (og[...].astype(F32) * (conv + sk[...] * gated[...].astype(F32))).astype(BF16)

    for ra in (2,):
        for h in (0, 1):
            w_wait(h, 1, ra, "R")
            w_send(h, 1, ra, "FR")
            w_wait(h, 1, ra, "L")
            w_send(h, 1, ra, "FL")
    for ra in (0, -1, 1, 2):
        for h in (0, 1):
            w_wait(h, 1, ra, "FR")
            w_wait(h, 1, ra, "FL")

    cols = w_h.shape[1]

    def columns(rx, c, n):
        q = lax.rem(x + rx + RING, RING)
        return jnp.dot(mix[...], wall[q * RING + c * 2 + n], preferred_element_type=F32)

    turns = (2, 1, -1, 0)
    swaps = []
    for k, rx in enumerate(turns):
        for n in (0, 1):
            other[k, :, n * cols : (n + 1) * cols] = columns(rx, 1 - core, n).astype(BF16)
        copy = pltpu.make_async_remote_copy(
            src_ref=other.at[k], dst_ref=cr.at[k], send_sem=osem_s.at[k], recv_sem=osem_r.at[k],
            device_id={"ch": ch_of(0, 1 - core)},
        )
        copy.start()
        swaps.append(copy)
    for k, rx in enumerate(turns):
        for n in (0, 1):
            part[k, :, n * cols : (n + 1) * cols] = columns(rx, core, n)

    rows = mix.shape[0]
    top, low = pl.ds(0, rows // 2), pl.ds(rows // 2, rows // 2)

    def ring(n, src, dst, step):
        copy = pltpu.make_async_remote_copy(
            src_ref=src, dst_ref=dst, send_sem=xsem_s.at[n], recv_sem=xsem_r.at[n],
            device_id={"ch": ch_of(step, core)},
        )
        copy.start()
        return copy

    swaps[0].wait_recv()
    s1[...] = (part[0] + cr[0].astype(F32)).astype(BF16)
    up1 = ring(0, s1.at[top], r1.at[top], 1)
    down1 = ring(1, s1.at[low], r1.at[low], -1)
    swaps[1].wait_recv()
    s2[0, low, :] = (part[1, low, :] + cr[1, low, :].astype(F32)).astype(BF16)
    up2 = ring(2, s2.at[0, low], r2.at[0, low], 1)
    swaps[2].wait_recv()
    s2[1, top, :] = (part[2, top, :] + cr[2, top, :].astype(F32)).astype(BF16)
    down2 = ring(3, s2.at[1, top], r2.at[1, top], -1)
    up1.wait_recv()
    s2[0, top, :] = (part[1, top, :] + cr[1, top, :].astype(F32) + r1[top, :].astype(F32)).astype(BF16)
    up3 = ring(4, s2.at[0, top], r2.at[0, top], 1)
    down1.wait_recv()
    s2[1, low, :] = (part[2, low, :] + cr[2, low, :].astype(F32) + r1[low, :].astype(F32)).astype(BF16)
    down3 = ring(5, s2.at[1, low], r2.at[1, low], -1)
    swaps[3].wait_recv()
    part[3] = part[3] + cr[3].astype(F32)
    for copy in (up2, down2, up3, down3):
        copy.wait_recv()
    out_ref[...] = (part[3] + r2[0].astype(F32) + r2[1].astype(F32)).astype(BF16)

    for copy in sent + swaps + [up1, down1, up2, down2, up3, down3]:
        copy.wait_send()


def per_device(outer_gate, inner_gate, values_in, filters, skip_gain, w_out):
    rows, chans = outer_gate.shape
    depth, cols = w_out.shape
    nctx = 16
    hbm = pl.BlockSpec(memory_space=pl.ANY)
    vmem = pl.BlockSpec(memory_space=pltpu.VMEM)
    dma = pltpu.SemaphoreType.DMA
    scratch = [
        pltpu.VMEM((rows, chans), BF16),
        pltpu.VMEM((rows, chans), BF16),
        pltpu.VMEM((rows, chans), BF16),
        pltpu.VMEM((rows, chans), F32),
        pltpu.VMEM((1, chans), F32),
        pltpu.VMEM((rows, 2 * rows), BF16),
        pltpu.VMEM((2 * rows, 2 * rows), BF16),
        pltpu.VMEM((rows, chans), BF16),
        pltpu.VMEM((chans, rows), BF16),
        pltpu.VMEM((chans, rows), BF16),
        pltpu.VMEM((chans, rows), BF16),
        pltpu.VMEM((chans, rows), BF16),
        pltpu.VMEM((chans, 2 * rows), F32),
        pltpu.VMEM((chans, 2 * rows), F32),
        pltpu.VMEM((chans, 2 * rows), F32),
        pltpu.VMEM((chans, 2 * rows), F32),
        pltpu.VMEM((chans, rows), BF16),
        pltpu.VMEM((chans, rows), BF16),
        pltpu.VMEM((rows, chans), BF16),
        pltpu.VMEM((nctx, depth, cols), BF16),
        pltpu.VMEM((RING, rows, 2 * cols), F32),
        pltpu.VMEM((RING, rows, 2 * cols), BF16),
        pltpu.VMEM((RING, rows, 2 * cols), BF16),
        pltpu.VMEM((rows, 2 * cols), BF16),
        pltpu.VMEM((rows, 2 * cols), BF16),
        pltpu.VMEM((2, rows, 2 * cols), BF16),
        pltpu.VMEM((2, rows, 2 * cols), BF16),
        dma((8,)),
        dma((nctx,)), dma((nctx,)), dma((nctx,)), dma((nctx,)), dma((nctx,)), dma((nctx,)),
        dma((40,)), dma((40,)),
        dma((RING,)), dma((RING,)),
        dma((6,)), dma((6,)),
    ]
    operands = (
        outer_gate, inner_gate, values_in, filters, skip_gain[None, :], w_out,
        jnp.asarray(forward_table(rows)), jnp.asarray(inverse_table(rows)),
    )
    return pl.pallas_call(
        kernel,
        out_shape=jax.ShapeDtypeStruct((rows, chans), BF16),
        in_specs=[hbm] * 8,
        out_specs=vmem,
        scratch_shapes=scratch,
        compiler_params=pltpu.CompilerParams(
            collective_id=0, has_side_effects=True, vmem_limit_bytes=48 * 1024 * 1024
        ),
        name="long_conv_layer",
    )(*[pltpu.with_memory_space_constraint(operand, pltpu.HBM) for operand in operands])


def solution(mesh):
    placed = (
        P("ctx", "ch"),
        P("ctx", "ch"),
        P("ctx", "ch"),
        P("ctx", "ch"),
        P("ch"),
        P("ch", "ctx"),
    )
    return jax.shard_map(
        per_device, mesh=mesh, in_specs=placed, out_specs=P("ctx", "ch"), check_vma=False
    )
```

```python
import functools

import jax
import jax.numpy as jnp
import numpy as np
from jax import lax
from jax.experimental import pallas as pl
from jax.experimental.pallas import tpu as pltpu
from jax.sharding import PartitionSpec as P

BF16 = jnp.bfloat16
F32 = jnp.float32
RING = 4


def forward_table(block):
    place = np.arange(block, dtype=np.int64)[:, None]
    freq = np.arange(block, dtype=np.int64)[None, :]
    angle = np.pi / (2 * block) * (place * (2 * freq + 1) % (4 * block)).astype(np.float64)
    return np.concatenate([np.cos(angle), -np.sin(angle)], axis=1).astype(jnp.bfloat16)


def inverse_table(block):
    freq = np.arange(block, dtype=np.int64)[:, None]
    place = np.arange(2 * block, dtype=np.int64)[None, :]
    angle = np.pi / (2 * block) * (place * (2 * freq + 1) % (4 * block)).astype(np.float64)
    return (np.concatenate([np.cos(angle), -np.sin(angle)], axis=0) / block).astype(jnp.bfloat16)


def kernel(
    og_h, ig_h, vi_h, fl_h, sk_h, w_h, ft_h, it_h, out_ref,
    og, ig, vi, fl, sk, ft, it, wl, gated, gsend, hsend, gx, hx, gs, hs, ys, ps, csend, cx, mixes, wall,
    part, other, cr, xs, xr,
    ld, gsem_s, gsem_r, hsem_s, hsem_r, csem_s, csem_r, wsem_s, wsem_r, psem_s, psem_r, osem_s, osem_r, xsem_s, xsem_r,
):
    nctx = 16
    me = lax.axis_index("ctx")
    mych = lax.axis_index("ch")
    y, z = lax.rem(me, RING), me // RING
    x, core = mych // 2, lax.rem(mych, 2)
    sub = gsend.shape[0] // nctx
    depth, cols = w_h.shape[0], w_h.shape[1]
    side = cols // 2
    odd = lax.rem(x, 2)
    partner = x + 1 - 2 * odd

    def ctx_of(ry, rz):
        return lax.rem(z + rz + RING, RING) * RING + lax.rem(y + ry + RING, RING)

    def ch_of(rx, c):
        return lax.rem(x + rx + RING, RING) * 2 + c

    loads = [
        pltpu.make_async_copy(src, dst, ld.at[n])
        for n, (src, dst) in enumerate(
            [(ig_h, ig), (vi_h, vi), (fl_h, fl), (w_h.at[:, pl.ds(pl.multiple_of(odd * side, side), side)], wall.at[me, 0]), (ft_h, ft), (it_h, it), (og_h, og), (sk_h, sk),
             (w_h.at[:, pl.ds(pl.multiple_of((1 - odd) * side, side), side)], wl)]
        )
    ]
    for copy in loads:
        copy.start()

    barrier = pltpu.get_barrier_semaphore()
    for d in range(1, nctx):
        pl.semaphore_signal(barrier, inc=1, device_id={"ctx": lax.rem(me + d, nctx)})
    pl.semaphore_signal(barrier, inc=1, device_id={"ch": ch_of(0, 1 - core)})
    for rx in (1, 2, 3):
        pl.semaphore_signal(barrier, inc=1, device_id={"ch": ch_of(rx, core)})

    sent = []
    kinds = {}

    def w_copy(h, stage, ra, what):
        key = (h, stage, ra, what)
        if key not in kinds:
            kinds[key] = len(kinds)
        n = kinds[key]
        step = 1 if what in ("R", "FR") else -1
        rel = {"R": 0, "L": 0, "FR": -1, "FL": 1}[what]
        rows = {"R": (0, depth), "L": (0, depth), "FR": (0, depth // 2), "FL": (depth // 2, depth // 2)}[what]
        first, second = (rel, 0) if stage == 0 else (ra, rel)
        chunk = ctx_of(first, second) if h == 0 else ctx_of(second, first)
        along_y = (h == 0) == (stage == 0)
        to = ctx_of(step, 0) if along_y else ctx_of(0, step)
        ref = wall.at[chunk, h, pl.ds(*rows)]
        return pltpu.make_async_remote_copy(
            src_ref=ref, dst_ref=ref, send_sem=wsem_s.at[n], recv_sem=wsem_r.at[n], device_id={"ctx": to}
        )

    def w_wait(h, stage, ra, what):
        n = kinds[(h, stage, ra, what)]
        step = 1 if what in ("R", "FR") else -1
        rel = {"R": 0, "L": 0, "FR": -1, "FL": 1}[what] - step
        rows = {"R": (0, depth), "L": (0, depth), "FR": (0, depth // 2), "FL": (depth // 2, depth // 2)}[what]
        first, second = (rel, 0) if stage == 0 else (ra, rel)
        chunk = ctx_of(first, second) if h == 0 else ctx_of(second, first)
        along_y = (h == 0) == (stage == 0)
        to = ctx_of(step, 0) if along_y else ctx_of(0, step)
        ref = wall.at[chunk, h, pl.ds(*rows)]
        pltpu.make_async_remote_copy(
            src_ref=ref, dst_ref=ref, send_sem=wsem_s.at[n], recv_sem=wsem_r.at[n], device_id={"ctx": to}
        ).wait_recv()

    def w_send(h, stage, ra, what):
        copy = w_copy(h, stage, ra, what)
        copy.start()
        sent.append(copy)

    def exchange(src, dst, ssem, rsem, d):
        to = lax.rem(me + d, nctx)
        return pltpu.make_async_remote_copy(
            src_ref=src.at[pl.ds(pl.multiple_of(to * sub, sub), sub)],
            dst_ref=dst.at[pl.ds(pl.multiple_of(me * sub, sub), sub)],
            send_sem=ssem.at[d],
            recv_sem=rsem.at[d],
            device_id={"ctx": to},
        )

    def exchange_wait(src, dst, ssem, rsem, d):
        frm = lax.rem(me - d + nctx, nctx)
        pltpu.make_async_remote_copy(
            src_ref=src.at[pl.ds(pl.multiple_of(frm * sub, sub), sub)],
            dst_ref=dst.at[pl.ds(pl.multiple_of(frm * sub, sub), sub)],
            send_sem=ssem.at[d],
            recv_sem=rsem.at[d],
            device_id={"ctx": frm},
        ).wait_recv()

    def exchange_all(src, dst, ssem, rsem):
        for d in range(1, nctx):
            copy = exchange(src, dst, ssem, rsem, d)
            copy.start()
            sent.append(copy)
        mine = pl.ds(pl.multiple_of(me * sub, sub), sub)
        dst[mine, :] = src[mine, :]

    loads[0].wait()
    loads[1].wait()
    product = (ig[...].astype(F32) * vi[...].astype(F32)).astype(BF16)
    gated[...] = product
    gsend[...] = jnp.transpose(product.astype(F32)).astype(BF16)
    loads[3].wait()
    pl.semaphore_wait(barrier, nctx + 3)
    loads[8].wait()

    def with_partner(n, src, dst):
        return pltpu.make_async_remote_copy(
            src_ref=src, dst_ref=dst, send_sem=psem_s.at[n], recv_sem=psem_r.at[n],
            device_id={"ch": partner * 2 + core},
        )

    w_pair = with_partner(0, wl, wall.at[me, 1])
    w_pair.start()
    sent.append(w_pair)
    exchange_all(gsend, gx, gsem_s, gsem_r)
    loads[2].wait()
    hsend[...] = jnp.transpose(fl[...]).astype(BF16)
    exchange_all(hsend, hx, hsem_s, hsem_r)
    for what in ("R", "L"):
        w_send(0, 0, 0, what)
    for what in ("R", "L"):
        w_send(0, 1, 0, what)
    w_pair.wait_recv()
    for what in ("R", "L"):
        w_send(1, 0, 0, what)
    for what in ("R", "L"):
        w_send(1, 1, 0, what)
    loads[4].wait()
    for d in range(1, nctx):
        exchange_wait(gsend, gx, gsem_s, gsem_r, d)
    gs[...] = jnp.dot(gx[...], ft[...], preferred_element_type=F32)
    for d in range(1, nctx):
        exchange_wait(hsend, hx, hsem_s, hsem_r, d)
    hs[...] = jnp.dot(hx[...], ft[...], preferred_element_type=F32)

    bins = gs.shape[1] // 2

    def block_products(n, carry):
        row = pl.multiple_of(n * 8, 8)
        for lane in range(0, bins, 128):
            gr = [gs[pl.ds(b * sub + row, 8), pl.ds(lane, 128)] for b in range(nctx)]
            gi = [gs[pl.ds(b * sub + row, 8), pl.ds(bins + lane, 128)] for b in range(nctx)]
            hr = [hs[pl.ds(b * sub + row, 8), pl.ds(lane, 128)] for b in range(nctx)]
            hi = [hs[pl.ds(b * sub + row, 8), pl.ds(bins + lane, 128)] for b in range(nctx)]
            for i in range(nctx):
                re = gr[0] * hr[i] - gi[0] * hi[i]
                im = gr[0] * hi[i] + gi[0] * hr[i]
                for j in range(1, i + 1):
                    re += gr[j] * hr[i - j] - gi[j] * hi[i - j]
                    im += gr[j] * hi[i - j] + gi[j] * hr[i - j]
                ys[pl.ds(i * sub + row, 8), pl.ds(lane, 128)] = re
                ys[pl.ds(i * sub + row, 8), pl.ds(bins + lane, 128)] = im
        return carry

    lax.fori_loop(0, sub // 8, block_products, 0)

    loads[5].wait()
    ps[...] = jnp.dot(ys[...].astype(BF16), it[...], preferred_element_type=F32)
    csend[pl.ds(0, sub), :] = ps[pl.ds(0, sub), pl.ds(0, bins)].astype(BF16)
    rest = sub * (nctx - 1)
    csend[pl.ds(sub, rest), :] = (
        ps[pl.ds(sub, rest), pl.ds(0, bins)] + ps[pl.ds(0, rest), pl.ds(bins, bins)]
    ).astype(BF16)
    exchange_all(csend, cx, csem_s, csem_r)

    def relay(h, stage, ra):
        w_wait(h, stage, ra, "R")
        w_send(h, stage, ra, "FR")
        w_wait(h, stage, ra, "L")
        w_send(h, stage, ra, "FL")

    relay(1, 0, 0)
    relay(0, 1, 0)
    relay(0, 0, 0)
    for ra in (-1, 1):
        for what in ("R", "L"):
            for h in (0, 1):
                w_send(h, 1, ra, what)

    loads[6].wait()
    loads[7].wait()
    for d in range(1, nctx):
        exchange_wait(csend, cx, csem_s, csem_r, d)
    conv = jnp.transpose(cx[...].astype(F32))
    mixes[0] = (og[...].astype(F32) * (conv + sk[...] * gated[...].astype(F32))).astype(BF16)

    m_pair = with_partner(1, mixes.at[0], mixes.at[1])
    m_pair.start()
    sent.append(m_pair)
    turns = (2, 1, -1, 0)

    def group_of(ry):
        there = lax.rem(y + ry + RING, RING)
        return there, there // 2 == core, lax.rem(there, 2)

    def swap(n, k):
        return pltpu.make_async_remote_copy(
            src_ref=other.at[n, k], dst_ref=cr.at[n, k],
            send_sem=osem_s.at[n * RING + k], recv_sem=osem_r.at[n * RING + k],
            device_id={"ch": ch_of(0, 1 - core)},
        )

    def share(n, k):
        return pltpu.make_async_remote_copy(
            src_ref=xs.at[n, k], dst_ref=xr.at[n, k],
            send_sem=xsem_s.at[n * RING + k], recv_sem=xsem_r.at[n * RING + k],
            device_id={"ch": ch_of(turns[k], core)},
        )

    def multiply(ry):
        there, mine, n = group_of(ry)
        for k in (0, 2):
            value = None
            for h in (0, 1):
                two = [wall[lax.rem(x + turns[k + i] + RING, RING) * RING + there, h] for i in (0, 1)]
                term = jnp.dot(mixes[h], jnp.concatenate(two, axis=1), preferred_element_type=F32)
                value = term if value is None else value + term

            @pl.when(mine)
            def _():
                for i in (0, 1):
                    part[n, k + i] = value[:, i * side : (i + 1) * side]

            @pl.when(jnp.logical_not(mine))
            def _():
                for i in (0, 1):
                    other[n, k + i] = value[:, i * side : (i + 1) * side].astype(BF16)
                    swap(n, k + i).start()

    def spread(ry):
        there, mine, n = group_of(ry)

        @pl.when(mine)
        def _():
            for k in range(RING - 1):
                swap(n, k).wait_recv()
                xs[n, k] = (part[n, k] + cr[n, k].astype(F32)).astype(BF16)
                share(n, k).start()

    def finish(ry):
        there, mine, n = group_of(ry)

        @pl.when(mine)
        def _():
            swap(n, RING - 1).wait_recv()
            total = part[n, RING - 1] + cr[n, RING - 1].astype(F32)
            for k in range(RING - 1):
                share(n, k).wait_recv()
            total += xr[n, 0].astype(F32)
            beside = xr[n, 1].astype(F32) + xr[n, 2].astype(F32)
            out_ref[:, pl.ds(pl.multiple_of(n * cols + odd * side, side), side)] = total.astype(BF16)
            out_ref[:, pl.ds(pl.multiple_of(n * cols + (1 - odd) * side, side), side)] = beside.astype(BF16)

        @pl.when(mine)
        def _():
            for k in range(RING - 1):
                share(n, k).wait_send()

        @pl.when(jnp.logical_not(mine))
        def _():
            for k in range(RING):
                swap(n, k).wait_send()

    for what in ("FR", "FL"):
        w_wait(1, 0, 0, what)
        w_wait(0, 1, 0, what)
    m_pair.wait_recv()
    multiply(0)
    for what in ("R", "L"):
        w_send(1, 1, 2, what)
    for ra in (-1, 1):
        relay(0, 1, ra)
    for what in ("FR", "FL"):
        w_wait(0, 0, 0, what)
    for what in ("R", "L"):
        w_send(0, 1, 2, what)
    spread(0)
    for ra in (0, -1, 1):
        relay(1, 1, ra)
    finish(0)
    for ra in (-1, 1):
        for what in ("FR", "FL"):
            w_wait(0, 1, ra, what)
    relay(1, 1, 2)
    multiply(-1)
    multiply(1)
    relay(0, 1, 2)
    spread(-1)
    spread(1)
    for what in ("FR", "FL"):
        w_wait(0, 1, 2, what)
        for ra in (0, -1, 1, 2):
            w_wait(1, 1, ra, what)
    multiply(2)
    spread(2)
    finish(-1)
    finish(1)
    finish(2)
    for copy in sent:
        copy.wait_send()


def per_device(outer_gate, inner_gate, values_in, filters, skip_gain, w_out):
    rows, chans = outer_gate.shape
    depth, cols = w_out.shape
    nctx = 16
    hbm = pl.BlockSpec(memory_space=pl.ANY)
    vmem = pl.BlockSpec(memory_space=pltpu.VMEM)
    dma = pltpu.SemaphoreType.DMA
    scratch = [
        pltpu.VMEM((rows, chans), BF16),
        pltpu.VMEM((rows, chans), BF16),
        pltpu.VMEM((rows, chans), BF16),
        pltpu.VMEM((rows, chans), F32),
        pltpu.VMEM((1, chans), F32),
        pltpu.VMEM((rows, 2 * rows), BF16),
        pltpu.VMEM((2 * rows, 2 * rows), BF16),
        pltpu.VMEM((depth, cols // 2), BF16),
        pltpu.VMEM((rows, chans), BF16),
        pltpu.VMEM((chans, rows), BF16),
        pltpu.VMEM((chans, rows), BF16),
        pltpu.VMEM((chans, rows), BF16),
        pltpu.VMEM((chans, rows), BF16),
        pltpu.VMEM((chans, 2 * rows), F32),
        pltpu.VMEM((chans, 2 * rows), F32),
        pltpu.VMEM((chans, 2 * rows), F32),
        pltpu.VMEM((chans, 2 * rows), F32),
        pltpu.VMEM((chans, rows), BF16),
        pltpu.VMEM((chans, rows), BF16),
        pltpu.VMEM((2, rows, chans), BF16),
        pltpu.VMEM((nctx, 2, depth, cols // 2), BF16),
        pltpu.VMEM((2, RING, rows, cols // 2), F32),
        pltpu.VMEM((2, RING, rows, cols // 2), BF16),
        pltpu.VMEM((2, RING, rows, cols // 2), BF16),
        pltpu.VMEM((2, RING, rows, cols // 2), BF16),
        pltpu.VMEM((2, RING, rows, cols // 2), BF16),
        dma((9,)),
        dma((nctx,)), dma((nctx,)), dma((nctx,)), dma((nctx,)), dma((nctx,)), dma((nctx,)),
        dma((40,)), dma((40,)),
        dma((2,)), dma((2,)),
        dma((2 * RING,)), dma((2 * RING,)),
        dma((2 * RING,)), dma((2 * RING,)),
    ]
    operands = (
        outer_gate, inner_gate, values_in, filters, skip_gain[None, :], w_out,
        jnp.asarray(forward_table(rows)), jnp.asarray(inverse_table(rows)),
    )
    return pl.pallas_call(
        kernel,
        out_shape=jax.ShapeDtypeStruct((rows, chans), BF16),
        in_specs=[hbm] * 8,
        out_specs=vmem,
        scratch_shapes=scratch,
        compiler_params=pltpu.CompilerParams(
            collective_id=0, has_side_effects=True, vmem_limit_bytes=48 * 1024 * 1024
        ),
        name="long_conv_layer",
    )(*[pltpu.with_memory_space_constraint(operand, pltpu.HBM) for operand in operands])


def solution(mesh):
    placed = (
        P("ctx", "ch"),
        P("ctx", "ch"),
        P("ctx", "ch"),
        P("ctx", "ch"),
        P("ch"),
        P("ch", "ctx"),
    )
    return jax.shard_map(
        per_device, mesh=mesh, in_specs=placed, out_specs=P("ctx", "ch"), check_vma=False
    )
```

```python
import functools

import jax
import jax.numpy as jnp
import numpy as np
from jax import lax
from jax.experimental import pallas as pl
from jax.experimental.pallas import tpu as pltpu
from jax.sharding import PartitionSpec as P

BF16 = jnp.bfloat16
F32 = jnp.float32
RING = 4


def forward_table(block):
    place = np.arange(block, dtype=np.int64)[:, None]
    freq = np.arange(block, dtype=np.int64)[None, :]
    angle = np.pi / (2 * block) * (place * (2 * freq + 1) % (4 * block)).astype(np.float64)
    return np.concatenate([np.cos(angle), -np.sin(angle)], axis=1).astype(jnp.bfloat16)


def inverse_table(block):
    freq = np.arange(block, dtype=np.int64)[:, None]
    place = np.arange(2 * block, dtype=np.int64)[None, :]
    angle = np.pi / (2 * block) * (place * (2 * freq + 1) % (4 * block)).astype(np.float64)
    return (np.concatenate([np.cos(angle), -np.sin(angle)], axis=0) / block).astype(jnp.bfloat16)


def kernel(
    og_h, ig_h, vi_h, fl_h, sk_h, w_h, ft_h, it_h, out_ref,
    og, ig, vi, fl, sk, ft, it, wl, gated, gsend, hsend, gx, hx, gs, hs, ys, ps, csend, cx, mixes, wall,
    part, other, cr, xs, xr,
    ld, gsem_s, gsem_r, hsem_s, hsem_r, csem_s, csem_r, wsem_s, wsem_r, psem_s, psem_r, osem_s, osem_r, xsem_s, xsem_r,
):
    nctx = 16
    me = lax.axis_index("ctx")
    mych = lax.axis_index("ch")
    y, z = lax.rem(me, RING), me // RING
    x, core = mych // 2, lax.rem(mych, 2)
    sub = gsend.shape[0] // nctx
    depth, cols = w_h.shape[0], w_h.shape[1]
    side = cols // 2
    odd = lax.rem(x, 2)
    partner = x + 1 - 2 * odd

    def ctx_of(ry, rz):
        return lax.rem(z + rz + RING, RING) * RING + lax.rem(y + ry + RING, RING)

    def ch_of(rx, c):
        return lax.rem(x + rx + RING, RING) * 2 + c

    loads = [
        pltpu.make_async_copy(src, dst, ld.at[n])
        for n, (src, dst) in enumerate(
            [(ig_h, ig), (vi_h, vi), (fl_h, fl), (w_h.at[:, pl.ds(pl.multiple_of(odd * side, side), side)], wall.at[me, 0]), (ft_h, ft), (it_h, it), (og_h, og), (sk_h, sk),
             (w_h.at[:, pl.ds(pl.multiple_of((1 - odd) * side, side), side)], wl)]
        )
    ]
    for copy in loads:
        copy.start()

    barrier = pltpu.get_barrier_semaphore()
    for d in range(1, nctx):
        pl.semaphore_signal(barrier, inc=1, device_id={"ctx": lax.rem(me + d, nctx)})
    pl.semaphore_signal(barrier, inc=1, device_id={"ch": ch_of(0, 1 - core)})
    for rx in (1, 2, 3):
        pl.semaphore_signal(barrier, inc=1, device_id={"ch": ch_of(rx, core)})

    sent = []
    kinds = {}

    def w_copy(h, stage, ra, what):
        key = (h, stage, ra, what)
        if key not in kinds:
            kinds[key] = len(kinds)
        n = kinds[key]
        step = 1 if what in ("R", "FR") else -1
        rel = {"R": 0, "L": 0, "FR": -1, "FL": 1}[what]
        rows = {"R": (0, depth), "L": (0, depth), "FR": (0, depth // 2), "FL": (depth // 2, depth // 2)}[what]
        first, second = (rel, 0) if stage == 0 else (ra, rel)
        chunk = ctx_of(first, second) if h == 0 else ctx_of(second, first)
        along_y = (h == 0) == (stage == 0)
        to = ctx_of(step, 0) if along_y else ctx_of(0, step)
        ref = wall.at[chunk, h, pl.ds(*rows)]
        return pltpu.make_async_remote_copy(
            src_ref=ref, dst_ref=ref, send_sem=wsem_s.at[n], recv_sem=wsem_r.at[n], device_id={"ctx": to}
        )

    def w_wait(h, stage, ra, what):
        n = kinds[(h, stage, ra, what)]
        step = 1 if what in ("R", "FR") else -1
        rel = {"R": 0, "L": 0, "FR": -1, "FL": 1}[what] - step
        rows = {"R": (0, depth), "L": (0, depth), "FR": (0, depth // 2), "FL": (depth // 2, depth // 2)}[what]
        first, second = (rel, 0) if stage == 0 else (ra, rel)
        chunk = ctx_of(first, second) if h == 0 else ctx_of(second, first)
        along_y = (h == 0) == (stage == 0)
        to = ctx_of(step, 0) if along_y else ctx_of(0, step)
        ref = wall.at[chunk, h, pl.ds(*rows)]
        pltpu.make_async_remote_copy(
            src_ref=ref, dst_ref=ref, send_sem=wsem_s.at[n], recv_sem=wsem_r.at[n], device_id={"ctx": to}
        ).wait_recv()

    def w_send(h, stage, ra, what):
        copy = w_copy(h, stage, ra, what)
        copy.start()
        sent.append(copy)

    def exchange(src, dst, ssem, rsem, d):
        to = lax.rem(me + d, nctx)
        return pltpu.make_async_remote_copy(
            src_ref=src.at[pl.ds(pl.multiple_of(to * sub, sub), sub)],
            dst_ref=dst.at[pl.ds(pl.multiple_of(me * sub, sub), sub)],
            send_sem=ssem.at[d],
            recv_sem=rsem.at[d],
            device_id={"ctx": to},
        )

    def exchange_wait(src, dst, ssem, rsem, d):
        frm = lax.rem(me - d + nctx, nctx)
        pltpu.make_async_remote_copy(
            src_ref=src.at[pl.ds(pl.multiple_of(frm * sub, sub), sub)],
            dst_ref=dst.at[pl.ds(pl.multiple_of(frm * sub, sub), sub)],
            send_sem=ssem.at[d],
            recv_sem=rsem.at[d],
            device_id={"ctx": frm},
        ).wait_recv()

    def exchange_all(src, dst, ssem, rsem):
        for d in range(1, nctx):
            copy = exchange(src, dst, ssem, rsem, d)
            copy.start()
            sent.append(copy)
        mine = pl.ds(pl.multiple_of(me * sub, sub), sub)
        dst[mine, :] = src[mine, :]

    loads[0].wait()
    loads[1].wait()
    product = (ig[...].astype(F32) * vi[...].astype(F32)).astype(BF16)
    gated[...] = product
    gsend[...] = jnp.transpose(product.astype(F32)).astype(BF16)
    loads[3].wait()
    pl.semaphore_wait(barrier, nctx + 3)
    loads[8].wait()

    def with_partner(n, src, dst):
        return pltpu.make_async_remote_copy(
            src_ref=src, dst_ref=dst, send_sem=psem_s.at[n], recv_sem=psem_r.at[n],
            device_id={"ch": partner * 2 + core},
        )

    w_pair = with_partner(0, wl, wall.at[me, 1])
    w_pair.start()
    sent.append(w_pair)
    exchange_all(gsend, gx, gsem_s, gsem_r)
    loads[2].wait()
    hsend[...] = jnp.transpose(fl[...]).astype(BF16)
    exchange_all(hsend, hx, hsem_s, hsem_r)
    for what in ("R", "L"):
        w_send(0, 0, 0, what)
    for what in ("R", "L"):
        w_send(0, 1, 0, what)
    w_pair.wait_recv()
    for what in ("R", "L"):
        w_send(1, 0, 0, what)
    for what in ("R", "L"):
        w_send(1, 1, 0, what)
    loads[4].wait()
    for d in range(1, nctx):
        exchange_wait(gsend, gx, gsem_s, gsem_r, d)
    gs[...] = jnp.dot(gx[...], ft[...], preferred_element_type=F32)
    for d in range(1, nctx):
        exchange_wait(hsend, hx, hsem_s, hsem_r, d)
    hs[...] = jnp.dot(hx[...], ft[...], preferred_element_type=F32)

    bins = gs.shape[1] // 2

    def block_products(n, carry):
        row = pl.multiple_of(n * 8, 8)
        for lane in range(0, bins, 128):
            gr = [gs[pl.ds(b * sub + row, 8), pl.ds(lane, 128)] for b in range(nctx)]
            gi = [gs[pl.ds(b * sub + row, 8), pl.ds(bins + lane, 128)] for b in range(nctx)]
            hr = [hs[pl.ds(b * sub + row, 8), pl.ds(lane, 128)] for b in range(nctx)]
            hi = [hs[pl.ds(b * sub + row, 8), pl.ds(bins + lane, 128)] for b in range(nctx)]
            for i in range(nctx):
                re = gr[0] * hr[i] - gi[0] * hi[i]
                im = gr[0] * hi[i] + gi[0] * hr[i]
                for j in range(1, i + 1):
                    re += gr[j] * hr[i - j] - gi[j] * hi[i - j]
                    im += gr[j] * hi[i - j] + gi[j] * hr[i - j]
                ys[pl.ds(i * sub + row, 8), pl.ds(lane, 128)] = re
                ys[pl.ds(i * sub + row, 8), pl.ds(bins + lane, 128)] = im
        return carry

    lax.fori_loop(0, sub // 8, block_products, 0)

    loads[5].wait()
    ps[...] = jnp.dot(ys[...].astype(BF16), it[...], preferred_element_type=F32)
    csend[pl.ds(0, sub), :] = ps[pl.ds(0, sub), pl.ds(0, bins)].astype(BF16)
    rest = sub * (nctx - 1)
    csend[pl.ds(sub, rest), :] = (
        ps[pl.ds(sub, rest), pl.ds(0, bins)] + ps[pl.ds(0, rest), pl.ds(bins, bins)]
    ).astype(BF16)
    exchange_all(csend, cx, csem_s, csem_r)

    def relay(h, stage, ra):
        w_wait(h, stage, ra, "R")
        w_send(h, stage, ra, "FR")
        w_wait(h, stage, ra, "L")
        w_send(h, stage, ra, "FL")

    relay(1, 0, 0)
    relay(0, 1, 0)
    relay(0, 0, 0)
    for ra in (-1, 1):
        for what in ("R", "L"):
            for h in (0, 1):
                w_send(h, 1, ra, what)

    loads[6].wait()
    loads[7].wait()
    for d in range(1, nctx):
        exchange_wait(csend, cx, csem_s, csem_r, d)
    conv = jnp.transpose(cx[...].astype(F32))
    mixes[0] = (og[...].astype(F32) * (conv + sk[...] * gated[...].astype(F32))).astype(BF16)

    m_pair = with_partner(1, mixes.at[0], mixes.at[1])
    m_pair.start()
    sent.append(m_pair)
    turns = (2, 1, -1, 0)

    def group_of(ry):
        there = lax.rem(y + ry + RING, RING)
        return there, there // 2 == core, lax.rem(there, 2)

    def swap(n, k):
        return pltpu.make_async_remote_copy(
            src_ref=other.at[n, k], dst_ref=cr.at[n, k],
            send_sem=osem_s.at[n * RING + k], recv_sem=osem_r.at[n * RING + k],
            device_id={"ch": ch_of(0, 1 - core)},
        )

    def share(n, k):
        return pltpu.make_async_remote_copy(
            src_ref=xs.at[n, k], dst_ref=xr.at[n, k],
            send_sem=xsem_s.at[n * RING + k], recv_sem=xsem_r.at[n * RING + k],
            device_id={"ch": ch_of(turns[k], core)},
        )

    def multiply(ry):
        there, mine, n = group_of(ry)
        for k in (0, 2):
            value = None
            for h in (0, 1):
                two = [wall[lax.rem(x + turns[k + i] + RING, RING) * RING + there, h] for i in (0, 1)]
                term = jnp.dot(mixes[h], jnp.concatenate(two, axis=1), preferred_element_type=F32)
                value = term if value is None else value + term

            @pl.when(mine)
            def _():
                for i in (0, 1):
                    part[n, k + i] = value[:, i * side : (i + 1) * side]

            @pl.when(jnp.logical_not(mine))
            def _():
                for i in (0, 1):
                    other[n, k + i] = value[:, i * side : (i + 1) * side].astype(BF16)
                    swap(n, k + i).start()

    def spread(ry):
        there, mine, n = group_of(ry)

        @pl.when(mine)
        def _():
            for k in range(RING - 1):
                swap(n, k).wait_recv()
                xs[n, k] = (part[n, k] + cr[n, k].astype(F32)).astype(BF16)
                share(n, k).start()

    def finish(ry):
        there, mine, n = group_of(ry)

        @pl.when(mine)
        def _():
            swap(n, RING - 1).wait_recv()
            total = part[n, RING - 1] + cr[n, RING - 1].astype(F32)
            for k in range(RING - 1):
                share(n, k).wait_recv()
            total += xr[n, 0].astype(F32)
            beside = xr[n, 1].astype(F32) + xr[n, 2].astype(F32)
            out_ref[:, pl.ds(pl.multiple_of(n * cols + odd * side, side), side)] = total.astype(BF16)
            out_ref[:, pl.ds(pl.multiple_of(n * cols + (1 - odd) * side, side), side)] = beside.astype(BF16)

        @pl.when(mine)
        def _():
            for k in range(RING - 1):
                share(n, k).wait_send()

        @pl.when(jnp.logical_not(mine))
        def _():
            for k in range(RING):
                swap(n, k).wait_send()

    for what in ("FR", "FL"):
        w_wait(1, 0, 0, what)
    for what in ("R", "L"):
        w_send(1, 1, 2, what)
    for what in ("FR", "FL"):
        w_wait(0, 1, 0, what)
    m_pair.wait_recv()
    multiply(0)
    for ra in (-1, 1):
        relay(0, 1, ra)
    for what in ("FR", "FL"):
        w_wait(0, 0, 0, what)
    for what in ("R", "L"):
        w_send(0, 1, 2, what)
    for ra in (0, -1, 1):
        relay(1, 1, ra)
    spread(0)
    relay(1, 1, 2)
    relay(0, 1, 2)
    for ra in (-1, 1):
        for what in ("FR", "FL"):
            w_wait(0, 1, ra, what)
    multiply(-1)
    multiply(1)
    spread(-1)
    spread(1)
    for what in ("FR", "FL"):
        w_wait(0, 1, 2, what)
        for ra in (0, -1, 1, 2):
            w_wait(1, 1, ra, what)
    multiply(2)
    spread(2)
    finish(0)
    finish(-1)
    finish(1)
    finish(2)
    for copy in sent:
        copy.wait_send()


def per_device(outer_gate, inner_gate, values_in, filters, skip_gain, w_out):
    rows, chans = outer_gate.shape
    depth, cols = w_out.shape
    nctx = 16
    hbm = pl.BlockSpec(memory_space=pl.ANY)
    vmem = pl.BlockSpec(memory_space=pltpu.VMEM)
    dma = pltpu.SemaphoreType.DMA
    scratch = [
        pltpu.VMEM((rows, chans), BF16),
        pltpu.VMEM((rows, chans), BF16),
        pltpu.VMEM((rows, chans), BF16),
        pltpu.VMEM((rows, chans), F32),
        pltpu.VMEM((1, chans), F32),
        pltpu.VMEM((rows, 2 * rows), BF16),
        pltpu.VMEM((2 * rows, 2 * rows), BF16),
        pltpu.VMEM((depth, cols // 2), BF16),
        pltpu.VMEM((rows, chans), BF16),
        pltpu.VMEM((chans, rows), BF16),
        pltpu.VMEM((chans, rows), BF16),
        pltpu.VMEM((chans, rows), BF16),
        pltpu.VMEM((chans, rows), BF16),
        pltpu.VMEM((chans, 2 * rows), F32),
        pltpu.VMEM((chans, 2 * rows), F32),
        pltpu.VMEM((chans, 2 * rows), F32),
        pltpu.VMEM((chans, 2 * rows), F32),
        pltpu.VMEM((chans, rows), BF16),
        pltpu.VMEM((chans, rows), BF16),
        pltpu.VMEM((2, rows, chans), BF16),
        pltpu.VMEM((nctx, 2, depth, cols // 2), BF16),
        pltpu.VMEM((2, RING, rows, cols // 2), F32),
        pltpu.VMEM((2, RING, rows, cols // 2), BF16),
        pltpu.VMEM((2, RING, rows, cols // 2), BF16),
        pltpu.VMEM((2, RING, rows, cols // 2), BF16),
        pltpu.VMEM((2, RING, rows, cols // 2), BF16),
        dma((9,)),
        dma((nctx,)), dma((nctx,)), dma((nctx,)), dma((nctx,)), dma((nctx,)), dma((nctx,)),
        dma((40,)), dma((40,)),
        dma((2,)), dma((2,)),
        dma((2 * RING,)), dma((2 * RING,)),
        dma((2 * RING,)), dma((2 * RING,)),
    ]
    operands = (
        outer_gate, inner_gate, values_in, filters, skip_gain[None, :], w_out,
        jnp.asarray(forward_table(rows)), jnp.asarray(inverse_table(rows)),
    )
    return pl.pallas_call(
        kernel,
        out_shape=jax.ShapeDtypeStruct((rows, chans), BF16),
        in_specs=[hbm] * 8,
        out_specs=vmem,
        scratch_shapes=scratch,
        compiler_params=pltpu.CompilerParams(
            collective_id=0, has_side_effects=True, vmem_limit_bytes=48 * 1024 * 1024
        ),
        name="long_conv_layer",
    )(*[pltpu.with_memory_space_constraint(operand, pltpu.HBM) for operand in operands])


def solution(mesh):
    placed = (
        P("ctx", "ch"),
        P("ctx", "ch"),
        P("ctx", "ch"),
        P("ctx", "ch"),
        P("ch"),
        P("ch", "ctx"),
    )
    return jax.shard_map(
        per_device, mesh=mesh, in_specs=placed, out_specs=P("ctx", "ch"), check_vma=False
    )
```

```python
import functools

import jax
import jax.numpy as jnp
import numpy as np
from jax import lax
from jax.experimental import pallas as pl
from jax.experimental.pallas import tpu as pltpu
from jax.sharding import PartitionSpec as P

BF16 = jnp.bfloat16
F32 = jnp.float32
RING = 4


def forward_table(block):
    place = np.arange(block, dtype=np.int64)[:, None]
    freq = np.arange(block, dtype=np.int64)[None, :]
    angle = np.pi / (2 * block) * (place * (2 * freq + 1) % (4 * block)).astype(np.float64)
    return np.concatenate([np.cos(angle), -np.sin(angle)], axis=1).astype(jnp.bfloat16)


def inverse_table(block):
    freq = np.arange(block, dtype=np.int64)[:, None]
    place = np.arange(2 * block, dtype=np.int64)[None, :]
    angle = np.pi / (2 * block) * (place * (2 * freq + 1) % (4 * block)).astype(np.float64)
    return (np.concatenate([np.cos(angle), -np.sin(angle)], axis=0) / block).astype(jnp.bfloat16)


def kernel(
    og_h, ig_h, vi_h, fl_h, sk_h, w_h, ft_h, it_h, out_ref,
    og, ig, vi, fl, sk, ft, it, wl, gated, gsend, hsend, gx, hx, gs, hs, ys, ps, csend, cx, mixes, wall,
    part, other, cr, xs, xr,
    ld, esem_s, esem_r, wsem_s, wsem_r, psem_s, psem_r, osem_s, osem_r, xsem_s, xsem_r,
):
    nctx = 16
    me = lax.axis_index("ctx")
    mych = lax.axis_index("ch")
    y, z = lax.rem(me, RING), me // RING
    x, core = mych // 2, lax.rem(mych, 2)
    sub = gsend.shape[0] // nctx
    depth, cols = w_h.shape[0], w_h.shape[1]
    side = cols // 2
    odd = lax.rem(x, 2)
    partner = x + 1 - 2 * odd

    along_y = [lax.rem(y + r, RING) for r in range(RING)]
    along_z = [lax.rem(z + r, RING) * RING for r in range(RING)]

    def ctx_of(ry, rz):
        return along_z[rz % RING] + along_y[ry % RING]

    def ch_of(rx, c):
        return lax.rem(x + rx + RING, RING) * 2 + c

    loads = [
        pltpu.make_async_copy(src, dst, ld.at[n])
        for n, (src, dst) in enumerate(
            [(ig_h, ig), (vi_h, vi), (fl_h, fl), (w_h.at[:, pl.ds(pl.multiple_of(odd * side, side), side)], wall.at[me, 0]), (ft_h, ft), (it_h, it), (og_h, og), (sk_h, sk),
             (w_h.at[:, pl.ds(pl.multiple_of((1 - odd) * side, side), side)], wl)]
        )
    ]
    for copy in loads:
        copy.start()

    barrier = pltpu.get_barrier_semaphore()
    others = [(ry, rz) for ry in (2, 1, 3, 0) for rz in (2, 1, 3, 0) if (ry, rz) != (0, 0)]
    for ry, rz in others:
        pl.semaphore_signal(barrier, inc=1, device_id={"ctx": ctx_of(ry, rz)})
    pl.semaphore_signal(barrier, inc=1, device_id={"ch": ch_of(0, 1 - core)})
    for rx in (1, 2, 3):
        pl.semaphore_signal(barrier, inc=1, device_id={"ch": ch_of(rx, core)})

    sent = []
    kinds = {}

    def w_copy(h, stage, ra, what):
        key = (h, stage, ra, what)
        if key not in kinds:
            kinds[key] = len(kinds)
        n = kinds[key]
        step = 1 if what in ("R", "FR") else -1
        rel = {"R": 0, "L": 0, "FR": -1, "FL": 1}[what]
        rows = {"R": (0, depth), "L": (0, depth), "FR": (0, depth // 2), "FL": (depth // 2, depth // 2)}[what]
        first, second = (rel, 0) if stage == 0 else (ra, rel)
        chunk = ctx_of(first, second) if h == 0 else ctx_of(second, first)
        to = ctx_of(step, 0) if (h == 0) == (stage == 0) else ctx_of(0, step)
        ref = wall.at[chunk, h, pl.ds(*rows)]
        return pltpu.make_async_remote_copy(
            src_ref=ref, dst_ref=ref, send_sem=wsem_s.at[0], recv_sem=wsem_r.at[n], device_id={"ctx": to}
        )

    def w_wait(h, stage, ra, what):
        n = kinds[(h, stage, ra, what)]
        step = 1 if what in ("R", "FR") else -1
        rel = {"R": 0, "L": 0, "FR": -1, "FL": 1}[what] - step
        rows = {"R": (0, depth), "L": (0, depth), "FR": (0, depth // 2), "FL": (depth // 2, depth // 2)}[what]
        first, second = (rel, 0) if stage == 0 else (ra, rel)
        chunk = ctx_of(first, second) if h == 0 else ctx_of(second, first)
        to = ctx_of(step, 0) if (h == 0) == (stage == 0) else ctx_of(0, step)
        ref = wall.at[chunk, h, pl.ds(*rows)]
        pltpu.make_async_remote_copy(
            src_ref=ref, dst_ref=ref, send_sem=wsem_s.at[0], recv_sem=wsem_r.at[n], device_id={"ctx": to}
        ).wait_recv()

    def w_send(h, stage, ra, what):
        w_copy(h, stage, ra, what).start()

    def exchange(src, dst, n):
        mine = pl.ds(pl.multiple_of(me * sub, sub), sub)
        for ry, rz in others:
            to = ctx_of(ry, rz)
            pltpu.make_async_remote_copy(
                src_ref=src.at[pl.ds(pl.multiple_of(to * sub, sub), sub)], dst_ref=dst.at[mine],
                send_sem=esem_s.at[n], recv_sem=esem_r.at[n], device_id={"ctx": to},
            ).start()
        dst[mine, :] = src[mine, :]

    def exchanged(src, dst, n):
        rest = pl.ds(0, (nctx - 1) * sub)
        return pltpu.make_async_remote_copy(
            src_ref=src.at[rest], dst_ref=dst.at[rest], send_sem=esem_s.at[n], recv_sem=esem_r.at[n],
            device_id={"ctx": lax.rem(me + 1, nctx)},
        )

    loads[0].wait()
    loads[1].wait()
    product = (ig[...].astype(F32) * vi[...].astype(F32)).astype(BF16)
    gated[...] = product
    gsend[...] = jnp.transpose(product.astype(F32)).astype(BF16)
    loads[3].wait()
    pl.semaphore_wait(barrier, nctx + 3)
    loads[8].wait()

    def with_partner(n, src, dst):
        return pltpu.make_async_remote_copy(
            src_ref=src, dst_ref=dst, send_sem=psem_s.at[n], recv_sem=psem_r.at[n],
            device_id={"ch": partner * 2 + core},
        )

    w_pair = with_partner(0, wl, wall.at[me, 1])
    w_pair.start()
    sent.append(w_pair)
    exchange(gsend, gx, 0)
    loads[2].wait()
    hsend[...] = jnp.transpose(fl[...]).astype(BF16)
    exchange(hsend, hx, 1)
    for what in ("R", "L"):
        w_send(0, 0, 0, what)
    for what in ("R", "L"):
        w_send(0, 1, 0, what)
    w_pair.wait_recv()
    for what in ("R", "L"):
        w_send(1, 0, 0, what)
    for what in ("R", "L"):
        w_send(1, 1, 0, what)
    loads[4].wait()
    exchanged(gsend, gx, 0).wait_recv()
    gs[...] = jnp.dot(gx[...], ft[...], preferred_element_type=F32)
    exchanged(hsend, hx, 1).wait_recv()
    hs[...] = jnp.dot(hx[...], ft[...], preferred_element_type=F32)

    bins = gs.shape[1] // 2

    def block_products(n, carry):
        row = pl.multiple_of(n * 8, 8)
        for lane in range(0, bins, 128):
            gr = [gs[pl.ds(b * sub + row, 8), pl.ds(lane, 128)] for b in range(nctx)]
            gi = [gs[pl.ds(b * sub + row, 8), pl.ds(bins + lane, 128)] for b in range(nctx)]
            hr = [hs[pl.ds(b * sub + row, 8), pl.ds(lane, 128)] for b in range(nctx)]
            hi = [hs[pl.ds(b * sub + row, 8), pl.ds(bins + lane, 128)] for b in range(nctx)]
            for i in range(nctx):
                re = gr[0] * hr[i] - gi[0] * hi[i]
                im = gr[0] * hi[i] + gi[0] * hr[i]
                for j in range(1, i + 1):
                    re += gr[j] * hr[i - j] - gi[j] * hi[i - j]
                    im += gr[j] * hi[i - j] + gi[j] * hr[i - j]
                ys[pl.ds(i * sub + row, 8), pl.ds(lane, 128)] = re
                ys[pl.ds(i * sub + row, 8), pl.ds(bins + lane, 128)] = im
        return carry

    lax.fori_loop(0, sub // 8, block_products, 0)

    loads[5].wait()
    ps[...] = jnp.dot(ys[...].astype(BF16), it[...], preferred_element_type=F32)
    csend[pl.ds(0, sub), :] = ps[pl.ds(0, sub), pl.ds(0, bins)].astype(BF16)
    rest = sub * (nctx - 1)
    csend[pl.ds(sub, rest), :] = (
        ps[pl.ds(sub, rest), pl.ds(0, bins)] + ps[pl.ds(0, rest), pl.ds(bins, bins)]
    ).astype(BF16)
    exchange(csend, cx, 2)

    def relay(h, stage, ra):
        w_wait(h, stage, ra, "R")
        w_send(h, stage, ra, "FR")
        w_wait(h, stage, ra, "L")
        w_send(h, stage, ra, "FL")

    relay(1, 0, 0)
    relay(0, 1, 0)
    relay(0, 0, 0)
    for ra in (-1, 1):
        for what in ("R", "L"):
            for h in (0, 1):
                w_send(h, 1, ra, what)

    loads[6].wait()
    loads[7].wait()
    exchanged(csend, cx, 2).wait_recv()
    conv = jnp.transpose(cx[...].astype(F32))
    mixes[0] = (og[...].astype(F32) * (conv + sk[...] * gated[...].astype(F32))).astype(BF16)

    m_pair = with_partner(1, mixes.at[0], mixes.at[1])
    m_pair.start()
    sent.append(m_pair)
    turns = (2, 1, -1, 0)

    def group_of(ry):
        there = along_y[ry % RING]
        return there, there // 2 == core, lax.rem(there, 2)

    def swap(n, k):
        return pltpu.make_async_remote_copy(
            src_ref=other.at[n, k], dst_ref=cr.at[n, k],
            send_sem=osem_s.at[n * RING + k], recv_sem=osem_r.at[n * RING + k],
            device_id={"ch": ch_of(0, 1 - core)},
        )

    def share(n, k):
        return pltpu.make_async_remote_copy(
            src_ref=xs.at[n, k], dst_ref=xr.at[n, k],
            send_sem=xsem_s.at[n * RING + k], recv_sem=xsem_r.at[n * RING + k],
            device_id={"ch": ch_of(turns[k], core)},
        )

    def multiply(ry):
        there, mine, n = group_of(ry)
        for k in (0, 2):
            value = None
            for h in (0, 1):
                two = [wall[lax.rem(x + turns[k + i] + RING, RING) * RING + there, h] for i in (0, 1)]
                term = jnp.dot(mixes[h], jnp.concatenate(two, axis=1), preferred_element_type=F32)
                value = term if value is None else value + term

            @pl.when(mine)
            def _():
                for i in (0, 1):
                    part[n, k + i] = value[:, i * side : (i + 1) * side]

            @pl.when(jnp.logical_not(mine))
            def _():
                for i in (0, 1):
                    other[n, k + i] = value[:, i * side : (i + 1) * side].astype(BF16)
                    swap(n, k + i).start()

    def spread(ry):
        there, mine, n = group_of(ry)

        @pl.when(mine)
        def _():
            for k in range(RING - 1):
                swap(n, k).wait_recv()
                xs[n, k] = (part[n, k] + cr[n, k].astype(F32)).astype(BF16)
                share(n, k).start()

    def finish(ry):
        there, mine, n = group_of(ry)

        @pl.when(mine)
        def _():
            swap(n, RING - 1).wait_recv()
            total = part[n, RING - 1] + cr[n, RING - 1].astype(F32)
            for k in range(RING - 1):
                share(n, k).wait_recv()
            total += xr[n, 0].astype(F32)
            beside = xr[n, 1].astype(F32) + xr[n, 2].astype(F32)
            out_ref[:, pl.ds(pl.multiple_of(n * cols + odd * side, side), side)] = total.astype(BF16)
            out_ref[:, pl.ds(pl.multiple_of(n * cols + (1 - odd) * side, side), side)] = beside.astype(BF16)

        @pl.when(mine)
        def _():
            for k in range(RING - 1):
                share(n, k).wait_send()

        @pl.when(jnp.logical_not(mine))
        def _():
            for k in range(RING):
                swap(n, k).wait_send()

    for what in ("FR", "FL"):
        w_wait(1, 0, 0, what)
    for what in ("R", "L"):
        w_send(1, 1, 2, what)
    for what in ("FR", "FL"):
        w_wait(0, 0, 0, what)
    for what in ("R", "L"):
        w_send(0, 1, 2, what)
    for ra in (-1, 1):
        relay(0, 1, ra)
    for ra in (0, -1, 1):
        relay(1, 1, ra)
    for what in ("FR", "FL"):
        w_wait(0, 1, 0, what)
    m_pair.wait_recv()
    multiply(0)
    spread(0)
    relay(1, 1, 2)
    relay(0, 1, 2)
    for ra in (-1, 1):
        for what in ("FR", "FL"):
            w_wait(0, 1, ra, what)
    multiply(-1)
    multiply(1)
    spread(-1)
    spread(1)
    exchanged(gsend, gx, 0).wait_send()
    exchanged(hsend, hx, 1).wait_send()
    exchanged(csend, cx, 2).wait_send()
    for copy in sent:
        copy.wait_send()
    for what in ("FR", "FL"):
        w_wait(0, 1, 2, what)
        for ra in (0, -1, 1, 2):
            w_wait(1, 1, ra, what)
    multiply(2)
    spread(2)
    finish(0)
    finish(-1)
    finish(1)
    finish(2)
    pltpu.make_async_remote_copy(
        src_ref=wall.at[pl.ds(0, nctx - 1)], dst_ref=wall.at[pl.ds(0, nctx - 1)], send_sem=wsem_s.at[0],
        recv_sem=wsem_r.at[0], device_id={"ctx": ctx_of(1, 0)},
    ).wait_send()


def per_device(outer_gate, inner_gate, values_in, filters, skip_gain, w_out):
    rows, chans = outer_gate.shape
    depth, cols = w_out.shape
    nctx = 16
    hbm = pl.BlockSpec(memory_space=pl.ANY)
    vmem = pl.BlockSpec(memory_space=pltpu.VMEM)
    dma = pltpu.SemaphoreType.DMA
    scratch = [
        pltpu.VMEM((rows, chans), BF16),
        pltpu.VMEM((rows, chans), BF16),
        pltpu.VMEM((rows, chans), BF16),
        pltpu.VMEM((rows, chans), F32),
        pltpu.VMEM((1, chans), F32),
        pltpu.VMEM((rows, 2 * rows), BF16),
        pltpu.VMEM((2 * rows, 2 * rows), BF16),
        pltpu.VMEM((depth, cols // 2), BF16),
        pltpu.VMEM((rows, chans), BF16),
        pltpu.VMEM((chans, rows), BF16),
        pltpu.VMEM((chans, rows), BF16),
        pltpu.VMEM((chans, rows), BF16),
        pltpu.VMEM((chans, rows), BF16),
        pltpu.VMEM((chans, 2 * rows), F32),
        pltpu.VMEM((chans, 2 * rows), F32),
        pltpu.VMEM((chans, 2 * rows), F32),
        pltpu.VMEM((chans, 2 * rows), F32),
        pltpu.VMEM((chans, rows), BF16),
        pltpu.VMEM((chans, rows), BF16),
        pltpu.VMEM((2, rows, chans), BF16),
        pltpu.VMEM((nctx, 2, depth, cols // 2), BF16),
        pltpu.VMEM((2, RING, rows, cols // 2), F32),
        pltpu.VMEM((2, RING, rows, cols // 2), BF16),
        pltpu.VMEM((2, RING, rows, cols // 2), BF16),
        pltpu.VMEM((2, RING, rows, cols // 2), BF16),
        pltpu.VMEM((2, RING, rows, cols // 2), BF16),
        dma((9,)),
        dma((3,)), dma((3,)),
        dma((1,)), dma((40,)),
        dma((2,)), dma((2,)),
        dma((2 * RING,)), dma((2 * RING,)),
        dma((2 * RING,)), dma((2 * RING,)),
    ]
    operands = (
        outer_gate, inner_gate, values_in, filters, skip_gain[None, :], w_out,
        jnp.asarray(forward_table(rows)), jnp.asarray(inverse_table(rows)),
    )
    return pl.pallas_call(
        kernel,
        out_shape=jax.ShapeDtypeStruct((rows, chans), BF16),
        in_specs=[hbm] * 8,
        out_specs=vmem,
        scratch_shapes=scratch,
        compiler_params=pltpu.CompilerParams(
            collective_id=0, has_side_effects=True, vmem_limit_bytes=48 * 1024 * 1024
        ),
        name="long_conv_layer",
    )(*[pltpu.with_memory_space_constraint(operand, pltpu.HBM) for operand in operands])


def solution(mesh):
    placed = (
        P("ctx", "ch"),
        P("ctx", "ch"),
        P("ctx", "ch"),
        P("ctx", "ch"),
        P("ch"),
        P("ch", "ctx"),
    )
    return jax.shard_map(
        per_device, mesh=mesh, in_specs=placed, out_specs=P("ctx", "ch"), check_vma=False
    )
```

```python
import functools

import jax
import jax.numpy as jnp
import numpy as np
from jax import lax
from jax.experimental import pallas as pl
from jax.experimental.pallas import tpu as pltpu
from jax.sharding import PartitionSpec as P

BF16 = jnp.bfloat16
F32 = jnp.float32
RING = 4


def forward_table(block):
    place = np.arange(block, dtype=np.int64)[:, None]
    freq = np.arange(block, dtype=np.int64)[None, :]
    angle = np.pi / (2 * block) * (place * (2 * freq + 1) % (4 * block)).astype(np.float64)
    return np.concatenate([np.cos(angle), -np.sin(angle)], axis=1).astype(jnp.bfloat16)


def inverse_table(block):
    freq = np.arange(block, dtype=np.int64)[:, None]
    place = np.arange(2 * block, dtype=np.int64)[None, :]
    angle = np.pi / (2 * block) * (place * (2 * freq + 1) % (4 * block)).astype(np.float64)
    return (np.concatenate([np.cos(angle), -np.sin(angle)], axis=0) / block).astype(jnp.bfloat16)


def kernel(
    og_h, ig_h, vi_h, fl_h, sk_h, w_h, ft_h, it_h, out_ref,
    og, ig, vi, fl, sk, ft, it, wl, gated, gsend, hsend, gx, hx, gs, hs, ys, ps, csend, cx, mixes, wall,
    part, other, cr, xs, xr, early,
    ld, esem_s, esem_r, wsem_s, wsem_r, psem_s, psem_r, osem_s, osem_r, xsem_s, xsem_r,
):
    nctx = 16
    me = lax.axis_index("ctx")
    mych = lax.axis_index("ch")
    y, z = lax.rem(me, RING), me // RING
    x, core = mych // 2, lax.rem(mych, 2)
    sub = gsend.shape[0] // nctx
    depth, cols = w_h.shape[0], w_h.shape[1]
    side = cols // 2
    odd = lax.rem(x, 2)
    partner = x + 1 - 2 * odd

    along_y = [lax.rem(y + r, RING) for r in range(RING)]
    along_z = [lax.rem(z + r, RING) * RING for r in range(RING)]

    def ctx_of(ry, rz):
        return along_z[rz % RING] + along_y[ry % RING]

    def ch_of(rx, c):
        return lax.rem(x + rx + RING, RING) * 2 + c

    loads = [
        pltpu.make_async_copy(src, dst, ld.at[n])
        for n, (src, dst) in enumerate(
            [(ig_h, ig), (vi_h, vi), (fl_h, fl), (w_h.at[:, pl.ds(pl.multiple_of(odd * side, side), side)], wall.at[me, 0]), (ft_h, ft), (it_h, it), (og_h, og), (sk_h, sk),
             (w_h.at[:, pl.ds(pl.multiple_of((1 - odd) * side, side), side)], wl)]
        )
    ]
    for copy in loads:
        copy.start()

    barrier = pltpu.get_barrier_semaphore()
    others = [(2, 2), (1, 2), (2, 1), (2, 3), (3, 2), (0, 2), (1, 1), (1, 3), (2, 0), (3, 1), (3, 3), (0, 1), (0, 3), (1, 0), (3, 0)]
    for ry, rz in others:
        pl.semaphore_signal(barrier, inc=1, device_id={"ctx": ctx_of(ry, rz)})
    pl.semaphore_signal(barrier, inc=1, device_id={"ch": ch_of(0, 1 - core)})
    for rx in (1, 2, 3):
        pl.semaphore_signal(barrier, inc=1, device_id={"ch": ch_of(rx, core)})

    sent = []
    kinds = {}

    def w_copy(h, stage, ra, what):
        key = (h, stage, ra, what)
        if key not in kinds:
            kinds[key] = len(kinds)
        n = kinds[key]
        step = 1 if what in ("R", "FR") else -1
        rel = {"R": 0, "L": 0, "FR": -1, "FL": 1}[what]
        rows = {"R": (0, depth), "L": (0, depth), "FR": (0, depth // 2), "FL": (depth // 2, depth // 2)}[what]
        first, second = (rel, 0) if stage == 0 else (ra, rel)
        chunk = ctx_of(first, second) if h == 0 else ctx_of(second, first)
        to = ctx_of(step, 0) if (h == 0) == (stage == 0) else ctx_of(0, step)
        ref = wall.at[chunk, h, pl.ds(*rows)]
        return pltpu.make_async_remote_copy(
            src_ref=ref, dst_ref=ref, send_sem=wsem_s.at[0], recv_sem=wsem_r.at[n], device_id={"ctx": to}
        )

    def w_wait(h, stage, ra, what):
        n = kinds[(h, stage, ra, what)]
        step = 1 if what in ("R", "FR") else -1
        rel = {"R": 0, "L": 0, "FR": -1, "FL": 1}[what] - step
        rows = {"R": (0, depth), "L": (0, depth), "FR": (0, depth // 2), "FL": (depth // 2, depth // 2)}[what]
        first, second = (rel, 0) if stage == 0 else (ra, rel)
        chunk = ctx_of(first, second) if h == 0 else ctx_of(second, first)
        to = ctx_of(step, 0) if (h == 0) == (stage == 0) else ctx_of(0, step)
        ref = wall.at[chunk, h, pl.ds(*rows)]
        pltpu.make_async_remote_copy(
            src_ref=ref, dst_ref=ref, send_sem=wsem_s.at[0], recv_sem=wsem_r.at[n], device_id={"ctx": to}
        ).wait_recv()

    def w_send(h, stage, ra, what):
        w_copy(h, stage, ra, what).start()

    def exchange(src, dst, n):
        mine = pl.ds(pl.multiple_of(me * sub, sub), sub)
        for ry, rz in others:
            to = ctx_of(ry, rz)
            pltpu.make_async_remote_copy(
                src_ref=src.at[pl.ds(pl.multiple_of(to * sub, sub), sub)], dst_ref=dst.at[mine],
                send_sem=esem_s.at[n], recv_sem=esem_r.at[n], device_id={"ctx": to},
            ).start()
        dst[mine, :] = src[mine, :]

    def exchanged(src, dst, n):
        rest = pl.ds(0, (nctx - 1) * sub)
        return pltpu.make_async_remote_copy(
            src_ref=src.at[rest], dst_ref=dst.at[rest], send_sem=esem_s.at[n], recv_sem=esem_r.at[n],
            device_id={"ctx": lax.rem(me + 1, nctx)},
        )

    loads[0].wait()
    loads[1].wait()
    product = (ig[...].astype(F32) * vi[...].astype(F32)).astype(BF16)
    gated[...] = product
    gsend[...] = jnp.transpose(product.astype(F32)).astype(BF16)
    loads[3].wait()
    pl.semaphore_wait(barrier, nctx + 3)
    loads[8].wait()

    def with_partner(n, src, dst):
        return pltpu.make_async_remote_copy(
            src_ref=src, dst_ref=dst, send_sem=psem_s.at[n], recv_sem=psem_r.at[n],
            device_id={"ch": partner * 2 + core},
        )

    w_pair = with_partner(0, wl, wall.at[me, 1])
    w_pair.start()
    sent.append(w_pair)
    exchange(gsend, gx, 0)
    loads[2].wait()
    hsend[...] = jnp.transpose(fl[...]).astype(BF16)
    exchange(hsend, hx, 1)
    for what in ("R", "L"):
        w_send(0, 0, 0, what)
    for what in ("R", "L"):
        w_send(0, 1, 0, what)
    w_pair.wait_recv()
    for what in ("R", "L"):
        w_send(1, 0, 0, what)
    for what in ("R", "L"):
        w_send(1, 1, 0, what)
    loads[4].wait()
    exchanged(gsend, gx, 0).wait_recv()
    gs[...] = jnp.dot(gx[...], ft[...], preferred_element_type=F32)
    exchanged(hsend, hx, 1).wait_recv()
    hs[...] = jnp.dot(hx[...], ft[...], preferred_element_type=F32)

    bins = gs.shape[1] // 2

    def block_products(n, carry):
        row = pl.multiple_of(n * 8, 8)
        for lane in range(0, bins, 128):
            gr = [gs[pl.ds(b * sub + row, 8), pl.ds(lane, 128)] for b in range(nctx)]
            gi = [gs[pl.ds(b * sub + row, 8), pl.ds(bins + lane, 128)] for b in range(nctx)]
            hr = [hs[pl.ds(b * sub + row, 8), pl.ds(lane, 128)] for b in range(nctx)]
            hi = [hs[pl.ds(b * sub + row, 8), pl.ds(bins + lane, 128)] for b in range(nctx)]
            for i in range(nctx):
                re = gr[0] * hr[i] - gi[0] * hi[i]
                im = gr[0] * hi[i] + gi[0] * hr[i]
                for j in range(1, i + 1):
                    re += gr[j] * hr[i - j] - gi[j] * hi[i - j]
                    im += gr[j] * hi[i - j] + gi[j] * hr[i - j]
                ys[pl.ds(i * sub + row, 8), pl.ds(lane, 128)] = re
                ys[pl.ds(i * sub + row, 8), pl.ds(bins + lane, 128)] = im
        return carry

    lax.fori_loop(0, sub // 8, block_products, 0)

    loads[5].wait()
    ps[...] = jnp.dot(ys[...].astype(BF16), it[...], preferred_element_type=F32)
    csend[pl.ds(0, sub), :] = ps[pl.ds(0, sub), pl.ds(0, bins)].astype(BF16)
    rest = sub * (nctx - 1)
    csend[pl.ds(sub, rest), :] = (
        ps[pl.ds(sub, rest), pl.ds(0, bins)] + ps[pl.ds(0, rest), pl.ds(bins, bins)]
    ).astype(BF16)
    exchange(csend, cx, 2)

    def relay(h, stage, ra):
        w_wait(h, stage, ra, "R")
        w_send(h, stage, ra, "FR")
        w_wait(h, stage, ra, "L")
        w_send(h, stage, ra, "FL")

    relay(1, 0, 0)
    relay(0, 1, 0)
    relay(0, 0, 0)
    for ra in (-1, 1):
        for what in ("R", "L"):
            for h in (0, 1):
                w_send(h, 1, ra, what)

    loads[6].wait()
    loads[7].wait()
    exchanged(csend, cx, 2).wait_recv()
    conv = jnp.transpose(cx[...].astype(F32))
    mixes[0] = (og[...].astype(F32) * (conv + sk[...] * gated[...].astype(F32))).astype(BF16)

    m_pair = with_partner(1, mixes.at[0], mixes.at[1])
    m_pair.start()
    sent.append(m_pair)
    turns = (2, 1, -1, 0)

    def group_of(ry):
        there = along_y[ry % RING]
        return there, there // 2 == core, lax.rem(there, 2)

    def swap(n, k):
        two = pl.ds(k, 2)
        return pltpu.make_async_remote_copy(
            src_ref=other.at[n, two], dst_ref=cr.at[n, two],
            send_sem=osem_s.at[n * RING + k], recv_sem=osem_r.at[n * RING + k],
            device_id={"ch": ch_of(0, 1 - core)},
        )

    def share(n, k):
        return pltpu.make_async_remote_copy(
            src_ref=xs.at[n, k], dst_ref=xr.at[n, k],
            send_sem=xsem_s.at[n * RING + k], recv_sem=xsem_r.at[n * RING + k],
            device_id={"ch": ch_of(turns[k], core)},
        )

    near_n = 1 - lax.rem(y, 2)

    def multiply_near(mine):
        there = (core if mine else 1 - core) * 2 + near_n
        for k in (0, 2):
            value = None
            for h in (0, 1):
                two = [wall[lax.rem(x + turns[k + i] + RING, RING) * RING + there, h] for i in (0, 1)]
                term = jnp.dot(mixes[h], jnp.concatenate(two, axis=1), preferred_element_type=F32)
                value = term if value is None else value + term
            for i in (0, 1):
                if mine:
                    part[near_n, k + i] = value[:, i * side : (i + 1) * side]
                else:
                    other[near_n, k + i] = value[:, i * side : (i + 1) * side].astype(BF16)
            if not mine:
                swap(near_n, k).start()

    def pass_on(n):
        for k in range(RING - 1):
            if k % 2 == 0:
                swap(n, k).wait_recv()
            xs[n, k] = (part[n, k] + cr[n, k].astype(F32)).astype(BF16)
            share(n, k).start()

    def multiply(ry):
        there, mine, n = group_of(ry)
        for k in (0, 2):
            value = None
            for h in (0, 1):
                two = [wall[lax.rem(x + turns[k + i] + RING, RING) * RING + there, h] for i in (0, 1)]
                term = jnp.dot(mixes[h], jnp.concatenate(two, axis=1), preferred_element_type=F32)
                value = term if value is None else value + term

            @pl.when(mine)
            def _():
                for i in (0, 1):
                    part[n, k + i] = value[:, i * side : (i + 1) * side]

            @pl.when(jnp.logical_not(mine))
            def _():
                for i in (0, 1):
                    other[n, k + i] = value[:, i * side : (i + 1) * side].astype(BF16)
                swap(n, k).start()

    def spread(ry):
        there, mine, n = group_of(ry)

        @pl.when(mine)
        def _():
            pass_on(n)

    def collect(n):
        total = part[n, RING - 1] + cr[n, RING - 1].astype(F32)
        for k in range(RING - 1):
            share(n, k).wait_recv()
        total += xr[n, 0].astype(F32)
        beside = xr[n, 1].astype(F32) + xr[n, 2].astype(F32)
        out_ref[:, pl.ds(pl.multiple_of(n * cols + odd * side, side), side)] = total.astype(BF16)
        out_ref[:, pl.ds(pl.multiple_of(n * cols + (1 - odd) * side, side), side)] = beside.astype(BF16)

    def finish(ry):
        there, mine, n = group_of(ry)

        @pl.when(mine)
        def _():
            collect(n)

        @pl.when(mine)
        def _():
            for k in range(RING - 1):
                share(n, k).wait_send()

        @pl.when(jnp.logical_not(mine))
        def _():
            for k in (0, 2):
                swap(n, k).wait_send()

    for what in ("FR", "FL"):
        w_wait(1, 0, 0, what)
    for what in ("R", "L"):
        w_send(1, 1, 2, what)
    for what in ("FR", "FL"):
        w_wait(0, 0, 0, what)
    for what in ("R", "L"):
        w_send(0, 1, 2, what)
    for ra in (-1, 1):
        relay(0, 1, ra)
    for ra in (0, -1, 1):
        relay(1, 1, ra)
    for what in ("FR", "FL"):
        w_wait(0, 1, 0, what)
    m_pair.wait_recv()
    multiply(0)
    spread(0)
    relay(1, 1, 2)
    relay(0, 1, 2)
    for ra in (-1, 1):
        for what in ("FR", "FL"):
            w_wait(0, 1, ra, what)
    multiply_near(False)
    multiply_near(True)
    pass_on(near_n)
    exchanged(gsend, gx, 0).wait_send()
    exchanged(hsend, hx, 1).wait_send()
    exchanged(csend, cx, 2).wait_send()
    for copy in sent:
        copy.wait_send()
    there, mine, n = group_of(2)

    def last_term(h, k):
        two = [wall[lax.rem(x + turns[k + i] + RING, RING) * RING + there, h] for i in (0, 1)]
        return jnp.dot(mixes[h], jnp.concatenate(two, axis=1), preferred_element_type=F32)

    for what in ("FR", "FL"):
        w_wait(0, 1, 2, what)
    early[0] = last_term(0, 0)
    early[1] = last_term(0, 2)
    for what in ("FR", "FL"):
        for ra in (0, -1, 1, 2):
            w_wait(1, 1, ra, what)
    for k in (0, 2):
        value = early[k // 2] + last_term(1, k)

        @pl.when(mine)
        def _():
            for i in (0, 1):
                part[n, k + i] = value[:, i * side : (i + 1) * side]

        @pl.when(jnp.logical_not(mine))
        def _():
            for i in (0, 1):
                other[n, k + i] = value[:, i * side : (i + 1) * side].astype(BF16)
            swap(n, k).start()

    spread(2)
    finish(0)
    collect(near_n)
    for k in (0, 2):
        swap(near_n, k).wait_send()
    for k in range(RING - 1):
        share(near_n, k).wait_send()
    finish(2)
    pltpu.make_async_remote_copy(
        src_ref=wall.at[pl.ds(0, nctx - 1)], dst_ref=wall.at[pl.ds(0, nctx - 1)], send_sem=wsem_s.at[0],
        recv_sem=wsem_r.at[0], device_id={"ctx": ctx_of(1, 0)},
    ).wait_send()


def per_device(outer_gate, inner_gate, values_in, filters, skip_gain, w_out):
    rows, chans = outer_gate.shape
    depth, cols = w_out.shape
    nctx = 16
    hbm = pl.BlockSpec(memory_space=pl.ANY)
    vmem = pl.BlockSpec(memory_space=pltpu.VMEM)
    dma = pltpu.SemaphoreType.DMA
    scratch = [
        pltpu.VMEM((rows, chans), BF16),
        pltpu.VMEM((rows, chans), BF16),
        pltpu.VMEM((rows, chans), BF16),
        pltpu.VMEM((rows, chans), F32),
        pltpu.VMEM((1, chans), F32),
        pltpu.VMEM((rows, 2 * rows), BF16),
        pltpu.VMEM((2 * rows, 2 * rows), BF16),
        pltpu.VMEM((depth, cols // 2), BF16),
        pltpu.VMEM((rows, chans), BF16),
        pltpu.VMEM((chans, rows), BF16),
        pltpu.VMEM((chans, rows), BF16),
        pltpu.VMEM((chans, rows), BF16),
        pltpu.VMEM((chans, rows), BF16),
        pltpu.VMEM((chans, 2 * rows), F32),
        pltpu.VMEM((chans, 2 * rows), F32),
        pltpu.VMEM((chans, 2 * rows), F32),
        pltpu.VMEM((chans, 2 * rows), F32),
        pltpu.VMEM((chans, rows), BF16),
        pltpu.VMEM((chans, rows), BF16),
        pltpu.VMEM((2, rows, chans), BF16),
        pltpu.VMEM((nctx, 2, depth, cols // 2), BF16),
        pltpu.VMEM((2, RING, rows, cols // 2), F32),
        pltpu.VMEM((2, RING, rows, cols // 2), BF16),
        pltpu.VMEM((2, RING, rows, cols // 2), BF16),
        pltpu.VMEM((2, RING, rows, cols // 2), BF16),
        pltpu.VMEM((2, RING, rows, cols // 2), BF16),
        pltpu.VMEM((2, rows, cols), F32),
        dma((9,)),
        dma((3,)), dma((3,)),
        dma((1,)), dma((40,)),
        dma((2,)), dma((2,)),
        dma((2 * RING,)), dma((2 * RING,)),
        dma((2 * RING,)), dma((2 * RING,)),
    ]
    operands = (
        outer_gate, inner_gate, values_in, filters, skip_gain[None, :], w_out,
        jnp.asarray(forward_table(rows)), jnp.asarray(inverse_table(rows)),
    )
    return pl.pallas_call(
        kernel,
        out_shape=jax.ShapeDtypeStruct((rows, chans), BF16),
        in_specs=[hbm] * 8,
        out_specs=vmem,
        scratch_shapes=scratch,
        compiler_params=pltpu.CompilerParams(
            collective_id=0, has_side_effects=True, vmem_limit_bytes=48 * 1024 * 1024
        ),
        name="long_conv_layer",
    )(*[pltpu.with_memory_space_constraint(operand, pltpu.HBM) for operand in operands])


def solution(mesh):
    placed = (
        P("ctx", "ch"),
        P("ctx", "ch"),
        P("ctx", "ch"),
        P("ctx", "ch"),
        P("ch"),
        P("ch", "ctx"),
    )
    return jax.shard_map(
        per_device, mesh=mesh, in_specs=placed, out_specs=P("ctx", "ch"), check_vma=False
    )
```

```python
import functools

import jax
import jax.numpy as jnp
import numpy as np
from jax import lax
from jax.experimental import pallas as pl
from jax.experimental.pallas import tpu as pltpu
from jax.sharding import PartitionSpec as P

BF16 = jnp.bfloat16
F32 = jnp.float32
RING = 4


def forward_table(block):
    place = np.arange(block, dtype=np.int64)[:, None]
    freq = np.arange(block, dtype=np.int64)[None, :]
    angle = np.pi / (2 * block) * (place * (2 * freq + 1) % (4 * block)).astype(np.float64)
    return np.concatenate([np.cos(angle), -np.sin(angle)], axis=1).astype(jnp.bfloat16)


def inverse_table(block):
    freq = np.arange(block, dtype=np.int64)[:, None]
    place = np.arange(2 * block, dtype=np.int64)[None, :]
    angle = np.pi / (2 * block) * (place * (2 * freq + 1) % (4 * block)).astype(np.float64)
    return (np.concatenate([np.cos(angle), -np.sin(angle)], axis=0) / block).astype(jnp.bfloat16)


def kernel(
    og_h, ig_h, vi_h, fl_h, sk_h, w_h, ft_h, it_h, out_ref,
    og, ig, vi, fl, sk, ft, it, wl, gated, gsend, hsend, gx, hx, gs, hs, ys, ps, csend, cx, mixes, wall,
    part, other, cr, xs, xr,
    ld, esem_s, esem_r, wsem_s, wsem_r, psem_s, psem_r, osem_s, osem_r, xsem_s, xsem_r,
):
    nctx = 16
    me = lax.axis_index("ctx")
    mych = lax.axis_index("ch")
    y, z = lax.rem(me, RING), me // RING
    x, core = mych // 2, lax.rem(mych, 2)
    sub = gsend.shape[0] // nctx
    depth, cols = w_h.shape[0], w_h.shape[1]
    side = cols // 2
    odd = lax.rem(x, 2)
    partner = x + 1 - 2 * odd

    along_y = [lax.rem(y + r, RING) for r in range(RING)]
    along_z = [lax.rem(z + r, RING) * RING for r in range(RING)]

    def ctx_of(ry, rz):
        return along_z[rz % RING] + along_y[ry % RING]

    def ch_of(rx, c):
        return lax.rem(x + rx + RING, RING) * 2 + c

    barrier = pltpu.get_barrier_semaphore()
    others = [(2, 2), (1, 2), (2, 1), (2, 3), (3, 2), (0, 2), (1, 1), (1, 3), (2, 0), (3, 1), (3, 3), (0, 1), (0, 3), (1, 0), (3, 0)]
    for ry, rz in others:
        pl.semaphore_signal(barrier, inc=1, device_id={"ctx": ctx_of(ry, rz)})
    pl.semaphore_signal(barrier, inc=1, device_id={"ch": ch_of(0, 1 - core)})
    for rx in (1, 2, 3):
        pl.semaphore_signal(barrier, inc=1, device_id={"ch": ch_of(rx, core)})

    loads = [
        pltpu.make_async_copy(src, dst, ld.at[n])
        for n, (src, dst) in enumerate(
            [(ig_h, ig), (vi_h, vi), (fl_h, fl), (w_h.at[:, pl.ds(pl.multiple_of(odd * side, side), side)], wall.at[me, 0]), (ft_h, ft), (it_h, it), (og_h, og), (sk_h, sk),
             (w_h.at[:, pl.ds(pl.multiple_of((1 - odd) * side, side), side)], wl)]
        )
    ]
    for copy in loads:
        copy.start()

    sent = []
    kinds = {}

    def w_copy(h, stage, ra, what):
        key = (h, stage, ra, what)
        if key not in kinds:
            kinds[key] = len(kinds)
        n = kinds[key]
        step = 1 if what in ("R", "FR") else -1
        rel = {"R": 0, "L": 0, "FR": -1, "FL": 1}[what]
        rows = {"R": (0, depth), "L": (0, depth), "FR": (0, depth // 2), "FL": (depth // 2, depth // 2)}[what]
        first, second = (rel, 0) if stage == 0 else (ra, rel)
        chunk = ctx_of(first, second) if h == 0 else ctx_of(second, first)
        to = ctx_of(step, 0) if (h == 0) == (stage == 0) else ctx_of(0, step)
        ref = wall.at[chunk, h, pl.ds(*rows)]
        return pltpu.make_async_remote_copy(
            src_ref=ref, dst_ref=ref, send_sem=wsem_s.at[0], recv_sem=wsem_r.at[n], device_id={"ctx": to}
        )

    def w_wait(h, stage, ra, what):
        n = kinds[(h, stage, ra, what)]
        step = 1 if what in ("R", "FR") else -1
        rel = {"R": 0, "L": 0, "FR": -1, "FL": 1}[what] - step
        rows = {"R": (0, depth), "L": (0, depth), "FR": (0, depth // 2), "FL": (depth // 2, depth // 2)}[what]
        first, second = (rel, 0) if stage == 0 else (ra, rel)
        chunk = ctx_of(first, second) if h == 0 else ctx_of(second, first)
        to = ctx_of(step, 0) if (h == 0) == (stage == 0) else ctx_of(0, step)
        ref = wall.at[chunk, h, pl.ds(*rows)]
        pltpu.make_async_remote_copy(
            src_ref=ref, dst_ref=ref, send_sem=wsem_s.at[0], recv_sem=wsem_r.at[n], device_id={"ctx": to}
        ).wait_recv()

    def w_send(h, stage, ra, what):
        w_copy(h, stage, ra, what).start()

    def exchange(src, dst, n):
        mine = pl.ds(pl.multiple_of(me * sub, sub), sub)
        for ry, rz in others:
            to = ctx_of(ry, rz)
            pltpu.make_async_remote_copy(
                src_ref=src.at[pl.ds(pl.multiple_of(to * sub, sub), sub)], dst_ref=dst.at[mine],
                send_sem=esem_s.at[n], recv_sem=esem_r.at[n], device_id={"ctx": to},
            ).start()
        dst[mine, :] = src[mine, :]

    def exchanged(src, dst, n):
        rest = pl.ds(0, (nctx - 1) * sub)
        return pltpu.make_async_remote_copy(
            src_ref=src.at[rest], dst_ref=dst.at[rest], send_sem=esem_s.at[n], recv_sem=esem_r.at[n],
            device_id={"ctx": lax.rem(me + 1, nctx)},
        )

    loads[0].wait()
    loads[1].wait()
    product = (ig[...].astype(F32) * vi[...].astype(F32)).astype(BF16)
    gated[...] = product
    gsend[...] = jnp.transpose(product.astype(F32)).astype(BF16)
    loads[3].wait()
    pl.semaphore_wait(barrier, nctx + 3)
    loads[8].wait()

    def with_partner(n, src, dst):
        return pltpu.make_async_remote_copy(
            src_ref=src, dst_ref=dst, send_sem=psem_s.at[n], recv_sem=psem_r.at[n],
            device_id={"ch": partner * 2 + core},
        )

    w_pair = with_partner(0, wl, wall.at[me, 1])
    w_pair.start()
    sent.append(w_pair)
    exchange(gsend, gx, 0)
    loads[2].wait()
    hsend[...] = jnp.transpose(fl[...]).astype(BF16)
    exchange(hsend, hx, 1)
    for what in ("R", "L"):
        w_send(0, 0, 0, what)
    for what in ("R", "L"):
        w_send(0, 1, 0, what)
    w_pair.wait_recv()
    for what in ("R", "L"):
        w_send(1, 0, 0, what)
    for what in ("R", "L"):
        w_send(1, 1, 0, what)
    loads[4].wait()
    exchanged(gsend, gx, 0).wait_recv()
    gs[...] = jnp.dot(gx[...], ft[...], preferred_element_type=F32)
    exchanged(hsend, hx, 1).wait_recv()
    hs[...] = jnp.dot(hx[...], ft[...], preferred_element_type=F32)

    bins = gs.shape[1] // 2

    def block_products(n, carry):
        row = pl.multiple_of(n * 8, 8)
        for lane in range(0, bins, 128):
            gr = [gs[pl.ds(b * sub + row, 8), pl.ds(lane, 128)] for b in range(nctx)]
            gi = [gs[pl.ds(b * sub + row, 8), pl.ds(bins + lane, 128)] for b in range(nctx)]
            hr = [hs[pl.ds(b * sub + row, 8), pl.ds(lane, 128)] for b in range(nctx)]
            hi = [hs[pl.ds(b * sub + row, 8), pl.ds(bins + lane, 128)] for b in range(nctx)]
            for i in range(nctx):
                re = gr[0] * hr[i] - gi[0] * hi[i]
                im = gr[0] * hi[i] + gi[0] * hr[i]
                for j in range(1, i + 1):
                    re += gr[j] * hr[i - j] - gi[j] * hi[i - j]
                    im += gr[j] * hi[i - j] + gi[j] * hr[i - j]
                ys[pl.ds(i * sub + row, 8), pl.ds(lane, 128)] = re
                ys[pl.ds(i * sub + row, 8), pl.ds(bins + lane, 128)] = im
        return carry

    lax.fori_loop(0, sub // 8, block_products, 0)

    loads[5].wait()
    ps[...] = jnp.dot(ys[...].astype(BF16), it[...], preferred_element_type=F32)
    csend[pl.ds(0, sub), :] = ps[pl.ds(0, sub), pl.ds(0, bins)].astype(BF16)
    rest = sub * (nctx - 1)
    csend[pl.ds(sub, rest), :] = (
        ps[pl.ds(sub, rest), pl.ds(0, bins)] + ps[pl.ds(0, rest), pl.ds(bins, bins)]
    ).astype(BF16)
    exchange(csend, cx, 2)

    def relay(h, stage, ra):
        w_wait(h, stage, ra, "R")
        w_send(h, stage, ra, "FR")
        w_wait(h, stage, ra, "L")
        w_send(h, stage, ra, "FL")

    relay(1, 0, 0)
    relay(0, 0, 0)
    for ra in (-1, 1):
        for what in ("R", "L"):
            for h in (0, 1):
                w_send(h, 1, ra, what)
    relay(0, 1, 0)

    loads[6].wait()
    loads[7].wait()
    exchanged(csend, cx, 2).wait_recv()
    conv = jnp.transpose(cx[...].astype(F32))
    mixes[0] = (og[...].astype(F32) * (conv + sk[...] * gated[...].astype(F32))).astype(BF16)

    m_pair = with_partner(1, mixes.at[0], mixes.at[1])
    m_pair.start()
    sent.append(m_pair)
    turns = (2, 1, -1, 0)

    def group_of(ry):
        there = along_y[ry % RING]
        return there, there // 2 == core, lax.rem(there, 2)

    def swap(n, k):
        return pltpu.make_async_remote_copy(
            src_ref=other.at[n, k], dst_ref=cr.at[n, k],
            send_sem=osem_s.at[n * RING + k], recv_sem=osem_r.at[n * RING + k],
            device_id={"ch": ch_of(0, 1 - core)},
        )

    def share(n, k):
        return pltpu.make_async_remote_copy(
            src_ref=xs.at[n, k], dst_ref=xr.at[n, k],
            send_sem=xsem_s.at[n * RING + k], recv_sem=xsem_r.at[n * RING + k],
            device_id={"ch": ch_of(turns[k], core)},
        )

    near_n = 1 - lax.rem(y, 2)

    def multiply_near(mine):
        there = (core if mine else 1 - core) * 2 + near_n
        for k in (0, 2):
            value = None
            for h in (0, 1):
                two = [wall[lax.rem(x + turns[k + i] + RING, RING) * RING + there, h] for i in (0, 1)]
                term = jnp.dot(mixes[h], jnp.concatenate(two, axis=1), preferred_element_type=F32)
                value = term if value is None else value + term
            for i in (0, 1):
                if mine:
                    part[near_n, k + i] = value[:, i * side : (i + 1) * side]
                else:
                    other[near_n, k + i] = value[:, i * side : (i + 1) * side].astype(BF16)
                    swap(near_n, k + i).start()

    def pass_on(n):
        for k in range(RING - 1):
            swap(n, k).wait_recv()
            xs[n, k] = (part[n, k] + cr[n, k].astype(F32)).astype(BF16)
            share(n, k).start()

    def multiply(ry):
        there, mine, n = group_of(ry)
        for k in (0, 2):
            value = None
            for h in (0, 1):
                two = [wall[lax.rem(x + turns[k + i] + RING, RING) * RING + there, h] for i in (0, 1)]
                term = jnp.dot(mixes[h], jnp.concatenate(two, axis=1), preferred_element_type=F32)
                value = term if value is None else value + term

            @pl.when(mine)
            def _():
                for i in (0, 1):
                    part[n, k + i] = value[:, i * side : (i + 1) * side]

            @pl.when(jnp.logical_not(mine))
            def _():
                for i in (0, 1):
                    other[n, k + i] = value[:, i * side : (i + 1) * side].astype(BF16)
                    swap(n, k + i).start()

    def spread(ry):
        there, mine, n = group_of(ry)

        @pl.when(mine)
        def _():
            pass_on(n)

    def collect(n):
        swap(n, RING - 1).wait_recv()
        total = part[n, RING - 1] + cr[n, RING - 1].astype(F32)
        for k in range(RING - 1):
            share(n, k).wait_recv()
        total += xr[n, 0].astype(F32)
        beside = xr[n, 1].astype(F32) + xr[n, 2].astype(F32)
        out_ref[:, pl.ds(pl.multiple_of(n * cols + odd * side, side), side)] = total.astype(BF16)
        out_ref[:, pl.ds(pl.multiple_of(n * cols + (1 - odd) * side, side), side)] = beside.astype(BF16)

    def finish(ry):
        there, mine, n = group_of(ry)

        @pl.when(mine)
        def _():
            collect(n)

        @pl.when(mine)
        def _():
            for k in range(RING - 1):
                share(n, k).wait_send()

        @pl.when(jnp.logical_not(mine))
        def _():
            for k in range(RING):
                swap(n, k).wait_send()

    for what in ("FR", "FL"):
        w_wait(1, 0, 0, what)
    for what in ("R", "L"):
        w_send(1, 1, 2, what)
    for what in ("FR", "FL"):
        w_wait(0, 0, 0, what)
    for what in ("R", "L"):
        w_send(0, 1, 2, what)
    for ra in (-1, 1):
        relay(0, 1, ra)
    for ra in (0, -1, 1):
        relay(1, 1, ra)
    for what in ("FR", "FL"):
        w_wait(0, 1, 0, what)
    m_pair.wait_recv()
    multiply(0)
    spread(0)
    relay(1, 1, 2)
    relay(0, 1, 2)
    for ra in (-1, 1):
        for what in ("FR", "FL"):
            w_wait(0, 1, ra, what)
    multiply_near(False)
    multiply_near(True)
    pass_on(near_n)
    exchanged(gsend, gx, 0).wait_send()
    exchanged(hsend, hx, 1).wait_send()
    exchanged(csend, cx, 2).wait_send()
    for copy in sent:
        copy.wait_send()
    for what in ("FR", "FL"):
        w_wait(0, 1, 2, what)
        for ra in (0, -1, 1, 2):
            w_wait(1, 1, ra, what)
    multiply(2)
    spread(2)
    finish(0)
    collect(near_n)
    for k in range(RING):
        swap(near_n, k).wait_send()
    for k in range(RING - 1):
        share(near_n, k).wait_send()
    finish(2)
    pltpu.make_async_remote_copy(
        src_ref=wall.at[pl.ds(0, nctx - 1)], dst_ref=wall.at[pl.ds(0, nctx - 1)], send_sem=wsem_s.at[0],
        recv_sem=wsem_r.at[0], device_id={"ctx": ctx_of(1, 0)},
    ).wait_send()


def per_device(outer_gate, inner_gate, values_in, filters, skip_gain, w_out):
    rows, chans = outer_gate.shape
    depth, cols = w_out.shape
    nctx = 16
    hbm = pl.BlockSpec(memory_space=pl.ANY)
    vmem = pl.BlockSpec(memory_space=pltpu.VMEM)
    dma = pltpu.SemaphoreType.DMA
    scratch = [
        pltpu.VMEM((rows, chans), BF16),
        pltpu.VMEM((rows, chans), BF16),
        pltpu.VMEM((rows, chans), BF16),
        pltpu.VMEM((rows, chans), F32),
        pltpu.VMEM((1, chans), F32),
        pltpu.VMEM((rows, 2 * rows), BF16),
        pltpu.VMEM((2 * rows, 2 * rows), BF16),
        pltpu.VMEM((depth, cols // 2), BF16),
        pltpu.VMEM((rows, chans), BF16),
        pltpu.VMEM((chans, rows), BF16),
        pltpu.VMEM((chans, rows), BF16),
        pltpu.VMEM((chans, rows), BF16),
        pltpu.VMEM((chans, rows), BF16),
        pltpu.VMEM((chans, 2 * rows), F32),
        pltpu.VMEM((chans, 2 * rows), F32),
        pltpu.VMEM((chans, 2 * rows), F32),
        pltpu.VMEM((chans, 2 * rows), F32),
        pltpu.VMEM((chans, rows), BF16),
        pltpu.VMEM((chans, rows), BF16),
        pltpu.VMEM((2, rows, chans), BF16),
        pltpu.VMEM((nctx, 2, depth, cols // 2), BF16),
        pltpu.VMEM((2, RING, rows, cols // 2), F32),
        pltpu.VMEM((2, RING, rows, cols // 2), BF16),
        pltpu.VMEM((2, RING, rows, cols // 2), BF16),
        pltpu.VMEM((2, RING, rows, cols // 2), BF16),
        pltpu.VMEM((2, RING, rows, cols // 2), BF16),
        dma((9,)),
        dma((3,)), dma((3,)),
        dma((1,)), dma((40,)),
        dma((2,)), dma((2,)),
        dma((2 * RING,)), dma((2 * RING,)),
        dma((2 * RING,)), dma((2 * RING,)),
    ]
    operands = (
        outer_gate, inner_gate, values_in, filters, skip_gain[None, :], w_out,
        jnp.asarray(forward_table(rows)), jnp.asarray(inverse_table(rows)),
    )
    return pl.pallas_call(
        kernel,
        out_shape=jax.ShapeDtypeStruct((rows, chans), BF16),
        in_specs=[hbm] * 8,
        out_specs=vmem,
        scratch_shapes=scratch,
        compiler_params=pltpu.CompilerParams(
            collective_id=0, has_side_effects=True, vmem_limit_bytes=48 * 1024 * 1024
        ),
        name="long_conv_layer",
    )(*[pltpu.with_memory_space_constraint(operand, pltpu.HBM) for operand in operands])


def solution(mesh):
    placed = (
        P("ctx", "ch"),
        P("ctx", "ch"),
        P("ctx", "ch"),
        P("ctx", "ch"),
        P("ch"),
        P("ch", "ctx"),
    )
    return jax.shard_map(
        per_device, mesh=mesh, in_specs=placed, out_specs=P("ctx", "ch"), check_vma=False
    )
```

```python
import functools

import jax
import jax.numpy as jnp
import numpy as np
from jax import lax
from jax.experimental import pallas as pl
from jax.experimental.pallas import tpu as pltpu
from jax.sharding import PartitionSpec as P

BF16 = jnp.bfloat16
F32 = jnp.float32
RING = 4


def forward_table(block):
    place = np.arange(block, dtype=np.int64)[:, None]
    freq = np.arange(block, dtype=np.int64)[None, :]
    angle = np.pi / (2 * block) * (place * (2 * freq + 1) % (4 * block)).astype(np.float64)
    return np.concatenate([np.cos(angle), -np.sin(angle)], axis=1).astype(jnp.bfloat16)


def inverse_table(block):
    freq = np.arange(block, dtype=np.int64)[:, None]
    place = np.arange(2 * block, dtype=np.int64)[None, :]
    angle = np.pi / (2 * block) * (place * (2 * freq + 1) % (4 * block)).astype(np.float64)
    return (np.concatenate([np.cos(angle), -np.sin(angle)], axis=0) / block).astype(jnp.bfloat16)


def kernel(
    og_h, ig_h, vi_h, fl_h, sk_h, w_h, ft_h, it_h, out_ref,
    og, ig, vi, fl, sk, ft, it, wl, gated, gsend, hsend, gx, hx, gs, hs, ys, ps, csend, cx, mixes, wall,
    part, other, cr, xs, xr, early,
    ld, esem_s, esem_r, wsem_s, wsem_r, psem_s, psem_r, osem_s, osem_r, xsem_s, xsem_r,
):
    nctx = 16
    me = lax.axis_index("ctx")
    mych = lax.axis_index("ch")
    y, z = lax.rem(me, RING), me // RING
    x, core = mych // 2, lax.rem(mych, 2)
    sub = gsend.shape[0] // nctx
    depth, cols = w_h.shape[0], w_h.shape[1]
    side = cols // 2
    odd = lax.rem(x, 2)
    partner = x + 1 - 2 * odd

    along_y = [lax.rem(y + r, RING) for r in range(RING)]
    along_z = [lax.rem(z + r, RING) * RING for r in range(RING)]

    def ctx_of(ry, rz):
        return along_z[rz % RING] + along_y[ry % RING]

    def ch_of(rx, c):
        return lax.rem(x + rx + RING, RING) * 2 + c

    loads = [
        pltpu.make_async_copy(src, dst, ld.at[n])
        for n, (src, dst) in enumerate(
            [(ig_h, ig), (vi_h, vi), (fl_h, fl), (w_h.at[:, pl.ds(pl.multiple_of(odd * side, side), side)], wall.at[me, 0]), (ft_h, ft), (it_h, it), (og_h, og), (sk_h, sk),
             (w_h.at[:, pl.ds(pl.multiple_of((1 - odd) * side, side), side)], wl)]
        )
    ]
    for copy in loads:
        copy.start()

    barrier = pltpu.get_barrier_semaphore()
    others = [(2, 2), (1, 2), (2, 1), (2, 3), (3, 2), (0, 2), (1, 1), (1, 3), (2, 0), (3, 1), (3, 3), (0, 1), (0, 3), (1, 0), (3, 0)]
    for ry, rz in others:
        pl.semaphore_signal(barrier, inc=1, device_id={"ctx": ctx_of(ry, rz)})
    pl.semaphore_signal(barrier, inc=1, device_id={"ch": ch_of(0, 1 - core)})
    for rx in (1, 2, 3):
        pl.semaphore_signal(barrier, inc=1, device_id={"ch": ch_of(rx, core)})

    sent = []
    kinds = {}

    def w_copy(h, stage, ra, what):
        key = (h, stage, ra, what)
        if key not in kinds:
            kinds[key] = len(kinds)
        n = kinds[key]
        step = 1 if what in ("R", "FR") else -1
        rel = {"R": 0, "L": 0, "FR": -1, "FL": 1}[what]
        rows = {"R": (0, depth), "L": (0, depth), "FR": (0, depth // 2), "FL": (depth // 2, depth // 2)}[what]
        first, second = (rel, 0) if stage == 0 else (ra, rel)
        chunk = ctx_of(first, second) if h == 0 else ctx_of(second, first)
        to = ctx_of(step, 0) if (h == 0) == (stage == 0) else ctx_of(0, step)
        ref = wall.at[chunk, h, pl.ds(*rows)]
        return pltpu.make_async_remote_copy(
            src_ref=ref, dst_ref=ref, send_sem=wsem_s.at[0], recv_sem=wsem_r.at[n], device_id={"ctx": to}
        )

    def w_wait(h, stage, ra, what):
        n = kinds[(h, stage, ra, what)]
        step = 1 if what in ("R", "FR") else -1
        rel = {"R": 0, "L": 0, "FR": -1, "FL": 1}[what] - step
        rows = {"R": (0, depth), "L": (0, depth), "FR": (0, depth // 2), "FL": (depth // 2, depth // 2)}[what]
        first, second = (rel, 0) if stage == 0 else (ra, rel)
        chunk = ctx_of(first, second) if h == 0 else ctx_of(second, first)
        to = ctx_of(step, 0) if (h == 0) == (stage == 0) else ctx_of(0, step)
        ref = wall.at[chunk, h, pl.ds(*rows)]
        pltpu.make_async_remote_copy(
            src_ref=ref, dst_ref=ref, send_sem=wsem_s.at[0], recv_sem=wsem_r.at[n], device_id={"ctx": to}
        ).wait_recv()

    def w_send(h, stage, ra, what):
        w_copy(h, stage, ra, what).start()

    def exchange(src, dst, n):
        mine = pl.ds(pl.multiple_of(me * sub, sub), sub)
        for ry, rz in others:
            to = ctx_of(ry, rz)
            pltpu.make_async_remote_copy(
                src_ref=src.at[pl.ds(pl.multiple_of(to * sub, sub), sub)], dst_ref=dst.at[mine],
                send_sem=esem_s.at[n], recv_sem=esem_r.at[n], device_id={"ctx": to},
            ).start()
        dst[mine, :] = src[mine, :]

    def exchanged(src, dst, n):
        rest = pl.ds(0, (nctx - 1) * sub)
        return pltpu.make_async_remote_copy(
            src_ref=src.at[rest], dst_ref=dst.at[rest], send_sem=esem_s.at[n], recv_sem=esem_r.at[n],
            device_id={"ctx": lax.rem(me + 1, nctx)},
        )

    loads[0].wait()
    loads[1].wait()
    product = (ig[...].astype(F32) * vi[...].astype(F32)).astype(BF16)
    gated[...] = product
    gsend[...] = jnp.transpose(product.astype(F32)).astype(BF16)
    loads[3].wait()
    pl.semaphore_wait(barrier, nctx + 3)
    loads[8].wait()

    def with_partner(n, src, dst):
        return pltpu.make_async_remote_copy(
            src_ref=src, dst_ref=dst, send_sem=psem_s.at[n], recv_sem=psem_r.at[n],
            device_id={"ch": partner * 2 + core},
        )

    w_pair = with_partner(0, wl, wall.at[me, 1])
    w_pair.start()
    sent.append(w_pair)
    exchange(gsend, gx, 0)
    loads[2].wait()
    hsend[...] = jnp.transpose(fl[...]).astype(BF16)
    exchange(hsend, hx, 1)
    for what in ("R", "L"):
        w_send(0, 0, 0, what)
    for what in ("R", "L"):
        w_send(0, 1, 0, what)
    w_pair.wait_recv()
    for what in ("R", "L"):
        w_send(1, 0, 0, what)
    for what in ("R", "L"):
        w_send(1, 1, 0, what)
    loads[4].wait()
    exchanged(gsend, gx, 0).wait_recv()
    gs[...] = jnp.dot(gx[...], ft[...], preferred_element_type=F32)
    exchanged(hsend, hx, 1).wait_recv()
    hs[...] = jnp.dot(hx[...], ft[...], preferred_element_type=F32)

    bins = gs.shape[1] // 2

    def block_products(n, carry):
        row = pl.multiple_of(n * 8, 8)
        for lane in range(0, bins, 128):
            gr = [gs[pl.ds(b * sub + row, 8), pl.ds(lane, 128)] for b in range(nctx)]
            gi = [gs[pl.ds(b * sub + row, 8), pl.ds(bins + lane, 128)] for b in range(nctx)]
            hr = [hs[pl.ds(b * sub + row, 8), pl.ds(lane, 128)] for b in range(nctx)]
            hi = [hs[pl.ds(b * sub + row, 8), pl.ds(bins + lane, 128)] for b in range(nctx)]
            for i in range(nctx):
                re = gr[0] * hr[i] - gi[0] * hi[i]
                im = gr[0] * hi[i] + gi[0] * hr[i]
                for j in range(1, i + 1):
                    re += gr[j] * hr[i - j] - gi[j] * hi[i - j]
                    im += gr[j] * hi[i - j] + gi[j] * hr[i - j]
                ys[pl.ds(i * sub + row, 8), pl.ds(lane, 128)] = re
                ys[pl.ds(i * sub + row, 8), pl.ds(bins + lane, 128)] = im
        return carry

    lax.fori_loop(0, sub // 8, block_products, 0)

    loads[5].wait()
    ps[...] = jnp.dot(ys[...].astype(BF16), it[...], preferred_element_type=F32)
    csend[pl.ds(0, sub), :] = ps[pl.ds(0, sub), pl.ds(0, bins)].astype(BF16)
    rest = sub * (nctx - 1)
    csend[pl.ds(sub, rest), :] = (
        ps[pl.ds(sub, rest), pl.ds(0, bins)] + ps[pl.ds(0, rest), pl.ds(bins, bins)]
    ).astype(BF16)
    exchange(csend, cx, 2)

    def relay(h, stage, ra):
        w_wait(h, stage, ra, "R")
        w_send(h, stage, ra, "FR")
        w_wait(h, stage, ra, "L")
        w_send(h, stage, ra, "FL")

    relay(1, 0, 0)
    relay(0, 1, 0)
    relay(0, 0, 0)
    for ra in (-1, 1):
        for what in ("R", "L"):
            for h in (0, 1):
                w_send(h, 1, ra, what)

    loads[6].wait()
    loads[7].wait()
    exchanged(csend, cx, 2).wait_recv()
    conv = jnp.transpose(cx[...].astype(F32))
    mixes[0] = (og[...].astype(F32) * (conv + sk[...] * gated[...].astype(F32))).astype(BF16)

    m_pair = with_partner(1, mixes.at[0], mixes.at[1])
    m_pair.start()
    sent.append(m_pair)
    turns = (2, 1, -1, 0)

    def group_of(ry):
        there = along_y[ry % RING]
        return there, there // 2 == core, lax.rem(there, 2)

    def swap(n, k):
        return pltpu.make_async_remote_copy(
            src_ref=other.at[n, k], dst_ref=cr.at[n, k],
            send_sem=osem_s.at[n * RING + k], recv_sem=osem_r.at[n * RING + k],
            device_id={"ch": ch_of(0, 1 - core)},
        )

    def share(n, k):
        return pltpu.make_async_remote_copy(
            src_ref=xs.at[n, k], dst_ref=xr.at[n, k],
            send_sem=xsem_s.at[n * RING + k], recv_sem=xsem_r.at[n * RING + k],
            device_id={"ch": ch_of(turns[k], core)},
        )

    near_n = 1 - lax.rem(y, 2)

    def multiply_near(mine):
        there = (core if mine else 1 - core) * 2 + near_n
        for k in (0, 2):
            value = None
            for h in (0, 1):
                two = [wall[lax.rem(x + turns[k + i] + RING, RING) * RING + there, h] for i in (0, 1)]
                term = jnp.dot(mixes[h], jnp.concatenate(two, axis=1), preferred_element_type=F32)
                value = term if value is None else value + term
            for i in (0, 1):
                if mine:
                    part[near_n, k + i] = value[:, i * side : (i + 1) * side]
                else:
                    other[near_n, k + i] = value[:, i * side : (i + 1) * side].astype(BF16)
                    swap(near_n, k + i).start()

    def pass_on(n):
        for k in range(RING - 1):
            swap(n, k).wait_recv()
            xs[n, k] = (part[n, k] + cr[n, k].astype(F32)).astype(BF16)
            share(n, k).start()

    def multiply(ry):
        there, mine, n = group_of(ry)
        for k in (0, 2):
            value = None
            for h in (0, 1):
                two = [wall[lax.rem(x + turns[k + i] + RING, RING) * RING + there, h] for i in (0, 1)]
                term = jnp.dot(mixes[h], jnp.concatenate(two, axis=1), preferred_element_type=F32)
                value = term if value is None else value + term

            @pl.when(mine)
            def _():
                for i in (0, 1):
                    part[n, k + i] = value[:, i * side : (i + 1) * side]

            @pl.when(jnp.logical_not(mine))
            def _():
                for i in (0, 1):
                    other[n, k + i] = value[:, i * side : (i + 1) * side].astype(BF16)
                    swap(n, k + i).start()

    def spread(ry):
        there, mine, n = group_of(ry)

        @pl.when(mine)
        def _():
            pass_on(n)

    def collect(n):
        swap(n, RING - 1).wait_recv()
        total = part[n, RING - 1] + cr[n, RING - 1].astype(F32)
        for k in range(RING - 1):
            share(n, k).wait_recv()
        total += xr[n, 0].astype(F32)
        beside = xr[n, 1].astype(F32) + xr[n, 2].astype(F32)
        out_ref[:, pl.ds(pl.multiple_of(n * cols + odd * side, side), side)] = total.astype(BF16)
        out_ref[:, pl.ds(pl.multiple_of(n * cols + (1 - odd) * side, side), side)] = beside.astype(BF16)

    def finish(ry):
        there, mine, n = group_of(ry)

        @pl.when(mine)
        def _():
            collect(n)

        @pl.when(mine)
        def _():
            for k in range(RING - 1):
                share(n, k).wait_send()

        @pl.when(jnp.logical_not(mine))
        def _():
            for k in range(RING):
                swap(n, k).wait_send()

    for what in ("FR", "FL"):
        w_wait(1, 0, 0, what)
    for what in ("R", "L"):
        w_send(1, 1, 2, what)
    for what in ("FR", "FL"):
        w_wait(0, 0, 0, what)
    for what in ("R", "L"):
        w_send(0, 1, 2, what)
    for ra in (-1, 1):
        relay(0, 1, ra)
    for ra in (0, -1, 1):
        relay(1, 1, ra)
    for what in ("FR", "FL"):
        w_wait(0, 1, 0, what)
    m_pair.wait_recv()
    multiply(0)
    spread(0)
    relay(1, 1, 2)
    relay(0, 1, 2)
    for ra in (-1, 1):
        for what in ("FR", "FL"):
            w_wait(0, 1, ra, what)
    multiply_near(False)
    multiply_near(True)
    pass_on(near_n)
    exchanged(gsend, gx, 0).wait_send()
    exchanged(hsend, hx, 1).wait_send()
    exchanged(csend, cx, 2).wait_send()
    for copy in sent:
        copy.wait_send()
    there, mine, n = group_of(2)

    def last_term(h, k):
        two = [wall[lax.rem(x + turns[k + i] + RING, RING) * RING + there, h] for i in (0, 1)]
        return jnp.dot(mixes[h], jnp.concatenate(two, axis=1), preferred_element_type=F32)

    for what in ("FR", "FL"):
        w_wait(0, 1, 2, what)
    early[0] = last_term(0, 0)
    early[1] = last_term(0, 2)
    for what in ("FR", "FL"):
        for ra in (0, -1, 1, 2):
            w_wait(1, 1, ra, what)
    for k in (0, 2):
        value = early[k // 2] + last_term(1, k)

        @pl.when(mine)
        def _():
            for i in (0, 1):
                part[n, k + i] = value[:, i * side : (i + 1) * side]

        @pl.when(jnp.logical_not(mine))
        def _():
            for i in (0, 1):
                other[n, k + i] = value[:, i * side : (i + 1) * side].astype(BF16)
                swap(n, k + i).start()

    spread(2)
    finish(0)
    collect(near_n)
    for k in range(RING):
        swap(near_n, k).wait_send()
    for k in range(RING - 1):
        share(near_n, k).wait_send()
    finish(2)
    pltpu.make_async_remote_copy(
        src_ref=wall.at[pl.ds(0, nctx - 1)], dst_ref=wall.at[pl.ds(0, nctx - 1)], send_sem=wsem_s.at[0],
        recv_sem=wsem_r.at[0], device_id={"ctx": ctx_of(1, 0)},
    ).wait_send()


def per_device(outer_gate, inner_gate, values_in, filters, skip_gain, w_out):
    rows, chans = outer_gate.shape
    depth, cols = w_out.shape
    nctx = 16
    hbm = pl.BlockSpec(memory_space=pl.ANY)
    vmem = pl.BlockSpec(memory_space=pltpu.VMEM)
    dma = pltpu.SemaphoreType.DMA
    scratch = [
        pltpu.VMEM((rows, chans), BF16),
        pltpu.VMEM((rows, chans), BF16),
        pltpu.VMEM((rows, chans), BF16),
        pltpu.VMEM((rows, chans), F32),
        pltpu.VMEM((1, chans), F32),
        pltpu.VMEM((rows, 2 * rows), BF16),
        pltpu.VMEM((2 * rows, 2 * rows), BF16),
        pltpu.VMEM((depth, cols // 2), BF16),
        pltpu.VMEM((rows, chans), BF16),
        pltpu.VMEM((chans, rows), BF16),
        pltpu.VMEM((chans, rows), BF16),
        pltpu.VMEM((chans, rows), BF16),
        pltpu.VMEM((chans, rows), BF16),
        pltpu.VMEM((chans, 2 * rows), F32),
        pltpu.VMEM((chans, 2 * rows), F32),
        pltpu.VMEM((chans, 2 * rows), F32),
        pltpu.VMEM((chans, 2 * rows), F32),
        pltpu.VMEM((chans, rows), BF16),
        pltpu.VMEM((chans, rows), BF16),
        pltpu.VMEM((2, rows, chans), BF16),
        pltpu.VMEM((nctx, 2, depth, cols // 2), BF16),
        pltpu.VMEM((2, RING, rows, cols // 2), F32),
        pltpu.VMEM((2, RING, rows, cols // 2), BF16),
        pltpu.VMEM((2, RING, rows, cols // 2), BF16),
        pltpu.VMEM((2, RING, rows, cols // 2), BF16),
        pltpu.VMEM((2, RING, rows, cols // 2), BF16),
        pltpu.VMEM((2, rows, cols), F32),
        dma((9,)),
        dma((3,)), dma((3,)),
        dma((1,)), dma((40,)),
        dma((2,)), dma((2,)),
        dma((2 * RING,)), dma((2 * RING,)),
        dma((2 * RING,)), dma((2 * RING,)),
    ]
    operands = (
        outer_gate, inner_gate, values_in, filters, skip_gain[None, :], w_out,
        jnp.asarray(forward_table(rows)), jnp.asarray(inverse_table(rows)),
    )
    return pl.pallas_call(
        kernel,
        out_shape=jax.ShapeDtypeStruct((rows, chans), BF16),
        in_specs=[hbm] * 8,
        out_specs=vmem,
        scratch_shapes=scratch,
        compiler_params=pltpu.CompilerParams(
            collective_id=0, has_side_effects=True, vmem_limit_bytes=48 * 1024 * 1024
        ),
        name="long_conv_layer",
    )(*[pltpu.with_memory_space_constraint(operand, pltpu.HBM) for operand in operands])


def solution(mesh):
    placed = (
        P("ctx", "ch"),
        P("ctx", "ch"),
        P("ctx", "ch"),
        P("ctx", "ch"),
        P("ch"),
        P("ch", "ctx"),
    )
    return jax.shard_map(
        per_device, mesh=mesh, in_specs=placed, out_specs=P("ctx", "ch"), check_vma=False
    )
```
